256 devices in a mesh: grp: 16 (over z, core), leaf: 16 (over y, x).
Axes of the slice: x: 4, y: 4, z: 8, core: 2. Of those that a mesh axis runs over, the one named last changes fastest.
Arguments:
- near_tiles: float32 [512, 16, 256, 256], P(('grp', 'leaf')), may hold values from -0.15625 to 0.15625
- diag_tiles: float32 [512, 256, 256], P(('grp', 'leaf')), as said below
- near_index: int32 [512, 16], P(('grp', 'leaf')), may hold values from 0 to 511, as said below
- near_mask: int32 [512, 16], P(('grp', 'leaf')), may hold values from 0 to 1
- leaf_basis: float32 [512, 256, 256], P(('grp', 'leaf')), as said below
- level1_basis: float32 [256, 256, 256], P(('grp', 'leaf')), as said below
- level2_basis: float32 [32768, 256], P(('grp', 'leaf')), as said below
Outputs:
- leaf_factor: float32 [512, 128, 128], P(('grp', 'leaf'))
- level1_factor: float32 [256, 128, 128], P(('grp', 'leaf'))
- level2_factor: float32 [16384, 128], P(('grp', 'leaf'))
- top_schur: float32 [16384, 128], P(('grp', 'leaf'))
- top_coupling: float32 [16384, 512], P(('grp', 'leaf'))
- log_det: float32 [], replicated
The draws below stay inside these ranges and needn't reach their ends.
Inputs may be any that keep to these rules, and one draw needn't show every extreme that they name: `near_index`: slot t of row i names box i + o for distinct nonzero offsets o with |o| <= 8, clipped to the range of boxes; a live slot is never clipped. `diag_tiles`: each tile is symmetric and positive definite. `leaf_basis`: each tile is orthogonal. `level1_basis`: each tile is orthogonal. `level2_basis`: each group's 2 * 128 rows form an orthogonal matrix.
All inputs are finite; a program needn't handle non-finite values.
Results may differ from the reference program's by a relative error of at most 0.0003.
Values sent between devices are 32-bit elements; how exact they have to be, the bound alone decides.
A program may use at most 128 MiB of HBM per device.

```python
import jax
import jax.numpy as jnp
from jax import lax

LEAF = 256
RANK = 128
NEAR = 16
BOXES = 512
BOX1 = 256
BOX2 = 128


def near_lists(key):
    seeded = jax.random.fold_in(key, 7)
    scores = jax.random.randint(jax.random.fold_in(seeded, 1), (BOXES, NEAR), 0, 1 << 20) * NEAR
    scores = scores + jnp.arange(NEAR, dtype=jnp.int32)[None, :]
    order = jnp.argsort(scores, axis=1).astype(jnp.int32)
    middle = NEAR // 2
    offset = jnp.where(order < middle, order - middle, order - middle + 1)
    target = jnp.arange(BOXES, dtype=jnp.int32)[:, None] + offset
    inside = (target >= 0) & (target < BOXES)
    near_ids = jnp.clip(target, 0, BOXES - 1).astype(jnp.int32)
    keeping = jax.random.randint(jax.random.fold_in(seeded, 2), (BOXES, 1), 3, NEAR + 1)
    live = inside & (jnp.arange(NEAR, dtype=jnp.int32)[None, :] < keeping)
    return (near_ids, live.astype(jnp.int32))


def orthogonal(key, number, order):
    return jnp.linalg.qr(jax.random.normal(key, (number, order, order), jnp.float32))[0]


def draw_near_index(key, part):
    return near_lists(key)[0]


def draw_near_mask(key, part):
    return near_lists(key)[1]


def draw_diag_tiles(key, part):
    first_key = jax.random.fold_in(key, 21)
    noise = 0.02 * jax.random.normal(first_key, (BOXES, LEAF, LEAF), jnp.float32)
    lifted = 2.0 + jnp.zeros((BOXES, 1, 1), jnp.float32)
    return lifted * jnp.eye(LEAF, dtype=jnp.float32)[None] + 0.5 * (noise + jnp.swapaxes(noise, 1, 2))


def draw_leaf_basis(key, part):
    return orthogonal(jax.random.fold_in(key, 31), BOXES, LEAF)


def draw_level1_basis(key, part):
    return orthogonal(jax.random.fold_in(key, 41), BOX1, 2 * RANK)


def draw_level2_basis(key, part):
    return orthogonal(jax.random.fold_in(key, 51), BOX2, 2 * RANK).reshape(BOX2 * 2 * RANK, 2 * RANK)


def levels(key, extent, cuts, smallest, largest):
    loudness, own = 1.0, jax.random.fold_in(key, 6)
    for dim, blocks in cuts:
        steps = jnp.exp(jax.random.uniform(jax.random.fold_in(own, dim), (blocks,), jnp.float32, smallest / len(cuts), largest / len(cuts)))
        loudness = loudness * jnp.repeat(steps, extent[dim] // blocks).reshape([-1 if axis == dim else 1 for axis in range(len(extent))])
    return loudness


def scatter_about(stream_key, extent, deviation, bound, shards=(), kind=jnp.bfloat16):
    gain = levels(stream_key, extent, shards, -0.22, 0.18) if shards else 1.0
    values = jax.random.normal(stream_key, extent, jnp.float32) * deviation * gain
    return jnp.minimum(jnp.maximum(values, -bound), bound).astype(kind)


def setup_inputs(seed: int = 0) -> dict:
    key_list = jax.random.split(jax.random.key(seed), 8)
    return {
        "near_tiles": scatter_about(key_list[0], (BOXES, NEAR, LEAF, LEAF), 0.01, 0.15625, ((0, 256),), jnp.float32),
        "diag_tiles": draw_diag_tiles(jax.random.fold_in(key_list[7], 71), 0),
        "near_index": draw_near_index(jax.random.fold_in(key_list[7], 71), 0),
        "near_mask": draw_near_mask(jax.random.fold_in(key_list[7], 71), 0),
        "leaf_basis": draw_leaf_basis(jax.random.fold_in(key_list[7], 71), 0),
        "level1_basis": draw_level1_basis(jax.random.fold_in(key_list[7], 71), 0),
        "level2_basis": draw_level2_basis(jax.random.fold_in(key_list[7], 71), 0),
    }


highest = lax.Precision.HIGHEST

def product(left, right):
    return jnp.matmul(left, right, precision=highest)

def factor_box(diagonal, transform, skeleton):
    redundant = diagonal.shape[0] - skeleton
    symmetric = 0.5 * (diagonal + diagonal.T)
    turned = product(product(transform.T, symmetric), transform)
    factor = jnp.linalg.cholesky(turned[:redundant, :redundant])
    panel_block = jax.scipy.linalg.solve_triangular(factor, turned[:redundant, redundant:], lower=True)
    schur_block = turned[redundant:, redundant:] - product(panel_block.T, panel_block)
    return (factor, panel_block, schur_block)

def couple(near_block, transform, panel_block, factor, target):
    redundant = factor.shape[0]
    rotated = product(transform.T, product(near_block, target))
    carried = jax.scipy.linalg.solve_triangular(factor, rotated[:redundant], lower=True)
    return rotated[redundant:] - product(panel_block.T, carried)

def couple_slots(near_blocks, transform, panel_block, factor, targets):
    return jax.vmap(couple, in_axes=(0, None, None, None, 0))(near_blocks, transform, panel_block, factor, targets)

def assemble_parents(coupling, schur_block, near_ids, live_mask, leaf_ids, radius):
    number = coupling.shape[0]
    skeleton = coupling.shape[2]
    parent = leaf_ids // 2
    offset = near_ids // 2 - parent[:, None] + radius
    choose_box = (offset[:, :, None] == jnp.arange(2 * radius + 1, dtype=jnp.int32)[None, None, :]).astype(jnp.float32)
    choose_box = choose_box * live_mask.astype(jnp.float32)[:, :, None]
    choose_half = ((near_ids % 2)[:, :, None] == jnp.arange(2, dtype=jnp.int32)[None, None, :]).astype(jnp.float32)
    weights = choose_box[:, :, :, None] * choose_half[:, :, None, :]
    blocks = jnp.einsum('nsdb,nsij->ndbij', weights, coupling, precision=highest)
    own_half = ((leaf_ids % 2)[:, None] == jnp.arange(2, dtype=jnp.int32)[None, :]).astype(jnp.float32)
    blocks = blocks.at[:, radius].add(own_half[:, :, None, None] * schur_block[:, None])
    blocks = blocks.reshape(number // 2, 2, 2 * radius + 1, 2, skeleton, skeleton).transpose(0, 2, 1, 4, 3, 5)
    return blocks.reshape(number // 2, 2 * radius + 1, 2 * skeleton, 2 * skeleton)

def level_couplings(blocks, transform, panel_block, factor, window, position, radius):
    offsets = [offset_slot for offset_slot in range(2 * radius + 1) if offset_slot != radius]
    targets = jnp.take(window, position + jnp.array(offsets, dtype=jnp.int32), axis=0)
    chosen = jnp.stack([blocks[offset_slot] for offset_slot in offsets])
    return couple_slots(chosen, transform, panel_block, factor, targets)

def assemble_top(coupling, schur_block):
    filler = jnp.zeros_like(schur_block[0])
    leaf_offsets = [-4, -3, -2, -1, 1, 2, 3, 4]
    slot_list = []
    for level_step in range(-2, 3):
        row_list = []
        for child_row in range(2):
            col_list = []
            for child_col in range(2):
                distance = 2 * level_step + child_col - child_row
                if distance == 0:
                    col_list.append(schur_block[child_row])
                elif distance in leaf_offsets:
                    col_list.append(coupling[child_row, leaf_offsets.index(distance)])
                else:
                    col_list.append(filler)
            row_list.append(jnp.concatenate(col_list, axis=1))
        slot_list.append(jnp.concatenate(row_list, axis=0))
    return jnp.stack(slot_list)

def log_sum(factor):
    return jnp.sum(jnp.log(jnp.diagonal(factor, axis1=-2, axis2=-1)))

def reference(near_tiles, diag_tiles, near_index, near_mask, leaf_basis, level1_basis, level2_basis):
    leaf_skeleton = leaf_basis[:, :, LEAF - RANK:]
    parent_window = jnp.pad(level1_basis[:, :, RANK:], ((4, 4), (0, 0), (0, 0)))

    def lower_levels(inputs):
        tiles, diagonals, near_ids, live_mask, transforms, parent_basis, parent = inputs
        leaf_ids = parent * 2 + jnp.arange(2, dtype=jnp.int32)
        leaf_lower, leaf_panel, leaf_schur = jax.vmap(factor_box, in_axes=(0, 0, None))(diagonals, transforms, RANK)
        targets = jnp.take(leaf_skeleton, near_ids.reshape(-1), axis=0).reshape(2, NEAR, LEAF, RANK)
        coupling = jax.vmap(couple_slots)(tiles, transforms, leaf_panel, leaf_lower, targets)
        coupling = coupling * live_mask.astype(jnp.float32)[:, :, None, None]
        blocks = assemble_parents(coupling, leaf_schur, near_ids, live_mask, leaf_ids, 4)[0]
        parent_lower, parent_panel, parent_schur = factor_box(blocks[4], parent_basis, RANK)
        parent_coupling = level_couplings(blocks, parent_basis, parent_panel, parent_lower, parent_window, parent, 4)
        return (leaf_lower, parent_lower, parent_schur, parent_coupling)
    inputs = (near_tiles.reshape(BOX1, 2, NEAR, LEAF, LEAF), diag_tiles.reshape(BOX1, 2, LEAF, LEAF), near_index.reshape(BOX1, 2, NEAR), near_mask.reshape(BOX1, 2, NEAR), leaf_basis.reshape(BOX1, 2, LEAF, LEAF), level1_basis, jnp.arange(BOX1, dtype=jnp.int32))
    leaf_lower, parent_lower, parent_schur, parent_coupling = lax.map(lower_levels, inputs)
    top_basis = level2_basis.reshape(BOX2, 2 * RANK, 2 * RANK)
    top_window = jnp.pad(top_basis[:, :, RANK:], ((2, 2), (0, 0), (0, 0)))

    def top_level(inputs):
        coupling, schur_pair, transform, group = inputs
        blocks = assemble_top(coupling, schur_pair)
        factor, panel_block, schur_block = factor_box(blocks[2], transform, RANK)
        group_coupling = level_couplings(blocks, transform, panel_block, factor, top_window, group, 2)
        return (factor, schur_block, group_coupling)
    top_lower, top_schur, top_coupling = lax.map(top_level, (parent_coupling.reshape(BOX2, 2, 8, RANK, RANK), parent_schur.reshape(BOX2, 2, RANK, RANK), top_basis, jnp.arange(BOX2, dtype=jnp.int32)))
    log_det = 2.0 * (log_sum(leaf_lower) + log_sum(parent_lower) + log_sum(top_lower))
    return (leaf_lower.reshape(BOXES, LEAF - RANK, LEAF - RANK), parent_lower, top_lower.reshape(BOX2 * RANK, RANK), top_schur.reshape(BOX2 * RANK, RANK), top_coupling.transpose(0, 2, 1, 3).reshape(BOX2 * RANK, 4 * RANK), log_det)
```

```python
import functools

import jax
import jax.numpy as jnp
from jax import lax
from jax.experimental import pallas as pl
from jax.experimental.pallas import tpu as pltpu
from jax.sharding import PartitionSpec as P

LEAF = 256
RANK = 128
NEAR = 16
AXES = ("grp", "leaf")
f32 = jnp.float32
bf16 = jnp.bfloat16
MESH = pl.DeviceIdType.MESH


def split(x):
    hi = x.astype(bf16)
    return hi, (x - hi.astype(f32)).astype(bf16)


def dg(a, b, ca, cb):
    return lax.dot_general(
        a, b, (((ca,), (cb,)), ((), ())), preferred_element_type=f32
    )


def dot3(a, b, ca=1, cb=0):
    ah, al = split(a)
    bh, bl = split(b)
    return dg(ah, bh, ca, cb) + (dg(ah, bl, ca, cb) + dg(al, bh, ca, cb))


def outer3(v, r):
    vh, vl = split(v)
    rh, rl = split(r)
    left = jnp.concatenate([vh, vl], axis=0)
    right = jnp.concatenate([rh, rh], axis=0)
    return dg(left, right, 0, 0) + dg(vh, rl, 0, 0)


def rowb(x, j):
    return jnp.broadcast_to(x[j : j + 1, :], x.shape)


def lane(x, i):
    return jnp.take_along_axis(x, jnp.full((8, 128), i, jnp.int32), axis=1)


def recip(b):
    r = pl.reciprocal(b, approx=True)
    r = r * (2.0 - b * r)
    return r * (2.0 - b * r)


def rsqrt(d):
    s = lax.rsqrt(d)
    return s * (1.5 - (0.5 * d) * (s * s))


def eliminate(A, VE, D, n):
    row = lax.broadcasted_iota(jnp.int32, (8, 128), 0)

    def body(k, carry):
        kk = pl.multiple_of(8 * k, 8)
        kn = pl.multiple_of(8 * jnp.minimum(k + 1, 15), 8)
        state = []
        for i in range(n):
            c0, c1, v0, v1, rr = carry[i]
            scaled = jnp.concatenate([v0 * rr, v1 * rr], axis=1)
            A[i] = A[i] - outer3(v0, scaled)
            nxt = A[i, pl.ds(kn, 8), :]
            n0, n1 = nxt[:, :128], nxt[:, 128:]
            cb = [lane(c0, kk + j) for j in range(8)]
            nb = [lane(n0, kk + j) for j in range(8)]
            one = jnp.ones_like(c0)
            state.append([c0, c1, n0, n1, cb, nb, c0, c1, one, one])
        for j in range(8):
            for i in range(n):
                x0, x1, n0, n1, cb, nb, v0, v1, d, rr = state[i]
                b = rowb(cb[j], j)
                r = recip(b)
                here = row == j
                m = jnp.where(here, 0.0, cb[j] * r)
                v0 = jnp.where(here, x0, v0)
                v1 = jnp.where(here, x1, v1)
                d = jnp.where(here, b, d)
                rr = jnp.where(here, r, rr)
                cb = [cb[q] - m * rowb(cb[q], j) if q > j else cb[q] for q in range(8)]
                x0 = x0 - m * rowb(x0, j)
                x1 = x1 - m * rowb(x1, j)
                state[i] = [x0, x1, n0, n1, cb, nb, v0, v1, d, rr]
        result = []
        for i in range(n):
            x0, x1, n0, n1, cb, nb, v0, v1, d, rr = state[i]
            p0, p1 = x0 * rr, x1 * rr
            for j in range(8):
                n0 = n0 - nb[j] * rowb(p0, j)
                n1 = n1 - nb[j] * rowb(p1, j)
            VE[i, pl.ds(kk, 8), :] = jnp.concatenate([v0, v1], axis=1)
            D[i, pl.ds(kk, 8), :] = d
            result.append((n0, n1, v0, v1, rr))
        return tuple(result)

    zero = jnp.zeros((8, 128), f32)
    start = tuple((A[i, 0:8, :128], A[i, 0:8, 128:], zero, zero, zero) for i in range(n))
    lax.fori_loop(0, 16, body, start)


def load_system(A, i, y_rr):
    rows = lax.broadcasted_iota(jnp.int32, (RANK, RANK), 0)
    cols = lax.broadcasted_iota(jnp.int32, (RANK, RANK), 1)
    A[i, :, :RANK] = y_rr
    A[i, :, RANK:] = (rows == cols).astype(f32)


def finish(VE, D, i, y, basis_t):
    rows = lax.broadcasted_iota(jnp.int32, (RANK, RANK), 0)
    cols = lax.broadcasted_iota(jnp.int32, (RANK, RANK), 1)
    d = D[i]
    s = rsqrt(d)
    upper = jnp.where(cols >= rows, VE[i, :, :RANK] * s, 0.0)
    inverse = VE[i, :, RANK:] * s
    xh = dot3(inverse, jnp.concatenate([y[:RANK, RANK:], basis_t[:RANK]], axis=1))
    sa = jnp.concatenate([y[RANK:, RANK:], basis_t[RANK:]], axis=1) - dot3(
        xh[:, :RANK], xh, 0, 0
    )
    return upper.T, sa[:, :RANK], sa[:, RANK:]


def log_rows(d):
    return jnp.sum(jnp.log(d), axis=0, keepdims=True)


def block_system(s0, c01, c10, s1):
    return jnp.concatenate(
        [
            jnp.concatenate([s0, 0.5 * (c01 + c10.T)], axis=1),
            jnp.concatenate([0.5 * (c01.T + c10), s1], axis=1),
        ],
        axis=0,
    )


def kernel(
    groups,
    leaves,
    near,
    diag,
    leaf_basis,
    basis1,
    basis2,
    ids,
    mask,
    F0,
    F1,
    F2,
    S2,
    C2,
    LD,
    nv,
    dv,
    bv,
    b1v,
    wv,
    bt,
    yv,
    tu,
    win,
    zown,
    zsib,
    zu,
    at,
    A,
    VE,
    D,
    ex,
    vf,
    f2,
    la,
    lg,
    load_sem,
    send_sem,
    recv_sem,
    la_send,
    la_recv,
    lg_send,
    lg_recv,
):
    count = groups * leaves
    g = lax.axis_index("grp")
    l = lax.axis_index("leaf")
    m = g * leaves + l
    par = lax.rem(m, 2)

    def device(k):
        return (k // leaves, lax.rem(k, leaves))

    def shifted(delta):
        return lax.rem(m + (delta + count), count)

    sibling = m + 1 - 2 * par

    loads = [
        pltpu.make_async_copy(leaf_basis, bv, load_sem.at[0]),
        pltpu.make_async_copy(basis1.at[0], b1v, load_sem.at[1]),
        pltpu.make_async_copy(basis2, wv.at[par], load_sem.at[2]),
        pltpu.make_async_copy(diag, dv, load_sem.at[3]),
        pltpu.make_async_copy(near, nv, load_sem.at[4]),
    ]
    for copy in loads:
        copy.start()

    barrier = pltpu.get_barrier_semaphore()
    deltas = (-1, 1, -2, 2, -3, 3, -4, 4)
    for delta in deltas:
        pl.semaphore_signal(barrier, inc=1, device_id=device(shifted(delta)), device_id_type=MESH)

    def greet_leaf(t, _):
        pl.semaphore_signal(
            barrier, inc=1, device_id=(g, lax.rem(l + t, leaves)), device_id_type=MESH
        )
        return 0

    def greet_group(t, _):
        pl.semaphore_signal(
            barrier, inc=1, device_id=(lax.rem(g + t, groups), l), device_id_type=MESH
        )
        return 0

    lax.fori_loop(1, leaves, greet_leaf, 0)
    lax.fori_loop(1, groups, greet_group, 0)

    for copy in loads[:3]:
        copy.wait()
    q2 = wv[par, :, RANK:]
    for b in range(2):
        t = dot3(bv[b, :, RANK:], b1v[b * RANK : (b + 1) * RANK, RANK:])
        tu[1, b] = t
        tu[0, b] = dot3(t, q2)

    pl.semaphore_wait(barrier, 8 + (leaves - 1) + (groups - 1))
    sends = []
    for k, delta in enumerate(deltas):
        target = shifted(delta)
        kind = jnp.where(target == sibling, 1, 0)
        sends.append(
            pltpu.make_async_remote_copy(
                src_ref=tu.at[kind],
                dst_ref=win.at[4 - delta],
                send_sem=send_sem.at[k],
                recv_sem=recv_sem.at[4 - delta],
                device_id=device(target),
                device_id_type=MESH,
            )
        )
    w_send = pltpu.make_async_remote_copy(
        src_ref=wv.at[par],
        dst_ref=wv.at[par],
        send_sem=send_sem.at[8],
        recv_sem=recv_sem.at[9],
        device_id=device(sibling),
        device_id_type=MESH,
    )
    w_send.start()
    for copy in sends:
        copy.start()

    loads[3].wait()
    for i in range(2):
        bt[i] = bv[i].T
        y = dot3(bt[i], dot3(dv[i], bv[i]))
        yv[i] = y
        load_system(A, i, y[:RANK, :RANK])
    eliminate(A, VE, D, 2)
    loads[4].wait()

    def near_block(a, j):
        slot = jnp.int32(0)
        live = f32(0.0)
        for t in range(NEAR):
            hit = jnp.logical_and(ids[a, t] == j, mask[a, t] == 1)
            slot = jnp.where(hit, t, slot)
            live = jnp.where(hit, f32(1.0), live)
        return nv[a * NEAR + slot], live

    schur = []
    logs = jnp.zeros((1, RANK), f32)
    for i in range(2):
        lower, s, a_t = finish(VE, D, i, yv[i], bt[i])
        F0[i] = lower
        at[i] = a_t
        schur.append(s)
        logs = logs + log_rows(D[i])
        tile, live = near_block(i, 2 * m + 1 - i)
        zown[i] = dot3(tile, bv[1 - i, :, RANK:] * live)

    system = block_system(schur[0], dot3(at[0], zown[0]), dot3(at[1], zown[1]), schur[1])
    bt[0] = b1v[...].T
    y = dot3(bt[0], dot3(system, b1v[...]))
    yv[0] = y
    load_system(A, 0, y[:RANK, :RANK])
    eliminate(A, VE, D, 1)

    def arrived(slot):
        pltpu.make_async_copy(win.at[slot], win.at[slot], recv_sem.at[slot]).wait()

    for delta in deltas:
        arrived(4 + delta)

    for i in range(2):
        z = jnp.zeros((LEAF, RANK), f32)
        for c in range(2):
            tile, live = near_block(i, 2 * sibling + c)
            z = z + dot3(tile, win[5 - 2 * par, c] * live)
        zsib[i * RANK : (i + 1) * RANK] = dot3(at[i], z)

    lower, s, a1_t = finish(VE, D, 0, yv[0], bt[0])
    F1[0] = lower
    logs = logs + log_rows(D[0])
    ex[par, 0] = s
    ex[par, 1] = dot3(a1_t, zsib[...])
    ex_send = pltpu.make_async_remote_copy(
        src_ref=ex.at[par],
        dst_ref=ex.at[par],
        send_sem=send_sem.at[9],
        recv_sem=recv_sem.at[10],
        device_id=device(sibling),
        device_id_type=MESH,
    )
    ex_send.start()

    def far(step, _):
        a = step // 4
        slot_e = lax.rem(step, 4)
        e = slot_e - 2 + slot_e // 2
        z = jnp.zeros((LEAF, RANK), f32)
        for c in range(4):
            tile, live = near_block(a, 4 * (m // 2) + 4 * e + c)
            source = jnp.clip(2 * e + c // 2 - par + 4, 0, 8)
            z = z + dot3(tile, win[source, c % 2] * live)
        zu[slot_e, pl.ds(pl.multiple_of(a * RANK, RANK), RANK)] = dot3(at[a], z)
        return 0

    win[4] = jnp.zeros((2, LEAF, RANK), f32)
    lax.fori_loop(0, 8, far, 0)
    vf[par] = dot3(a1_t, jnp.concatenate([zu[e] for e in range(4)], axis=1))
    v_send = pltpu.make_async_remote_copy(
        src_ref=vf.at[par],
        dst_ref=vf.at[par],
        send_sem=send_sem.at[10],
        recv_sem=recv_sem.at[11],
        device_id=device(sibling),
        device_id_type=MESH,
    )
    v_send.start()

    w_send.wait()
    w = jnp.concatenate([wv[0], wv[1]], axis=0)
    bt[0] = w.T
    ex_send.wait()
    system = block_system(ex[0, 0], ex[0, 1], ex[1, 1], ex[1, 0])
    y = dot3(bt[0], dot3(system, w))
    yv[0] = y
    load_system(A, 0, y[:RANK, :RANK])
    eliminate(A, VE, D, 1)
    logs = logs + log_rows(D[0]) * jnp.where(par == 0, 1.0, 0.0)
    la[l] = jnp.broadcast_to(logs, (8, RANK))

    def to_leaf(t, wait):
        copy = pltpu.make_async_remote_copy(
            src_ref=la.at[l],
            dst_ref=la.at[l],
            send_sem=la_send.at[t],
            recv_sem=la_recv.at[t],
            device_id=(g, lax.rem(l + t, leaves)),
            device_id_type=MESH,
        )
        if wait:
            copy.wait()
        else:
            copy.start()

    def to_group(t, wait):
        copy = pltpu.make_async_remote_copy(
            src_ref=lg.at[g],
            dst_ref=lg.at[g],
            send_sem=lg_send.at[t],
            recv_sem=lg_recv.at[t],
            device_id=(lax.rem(g + t, groups), l),
            device_id_type=MESH,
        )
        if wait:
            copy.wait()
        else:
            copy.start()

    def each(size, step, wait):
        def body(t, _):
            step(t, wait)
            return 0

        lax.fori_loop(1, size, body, 0)

    each(leaves, to_leaf, False)
    lower, s, a2_t = finish(VE, D, 0, yv[0], bt[0])
    half = pl.multiple_of(par * (RANK // 2), RANK // 2)
    f2[:, :RANK] = lower
    f2[:, RANK : 2 * RANK] = s
    f2[:, 2 * RANK :] = a2_t
    F2[...] = f2[pl.ds(half, RANK // 2), :RANK]
    S2[...] = f2[pl.ds(half, RANK // 2), RANK : 2 * RANK]
    each(leaves, to_leaf, True)
    lg[g] = jnp.sum(la[...], axis=0)
    each(groups, to_group, False)
    v_send.wait()
    C2[...] = dot3(
        f2[pl.ds(half, RANK // 2), 2 * RANK :], jnp.concatenate([vf[0], vf[1]], axis=0)
    )
    for copy in sends:
        copy.wait_send()
    each(groups, to_group, True)
    LD[...] = jnp.sum(lg[...], axis=0)


def on_device(
    near_tiles, diag_tiles, near_index, near_mask, leaf_basis, level1_basis, level2_basis
):
    groups, leaves = lax.axis_size("grp"), lax.axis_size("leaf")
    any_spec = pl.BlockSpec(memory_space=pl.ANY)
    smem = pl.BlockSpec(memory_space=pltpu.SMEM)
    vmem = pl.BlockSpec(memory_space=pltpu.VMEM)
    dma = pltpu.SemaphoreType.DMA
    outs = pl.pallas_call(
        functools.partial(kernel, groups, leaves),
        out_shape=(
            jax.ShapeDtypeStruct((2, RANK, RANK), f32),
            jax.ShapeDtypeStruct((1, RANK, RANK), f32),
            jax.ShapeDtypeStruct((RANK // 2, RANK), f32),
            jax.ShapeDtypeStruct((RANK // 2, RANK), f32),
            jax.ShapeDtypeStruct((RANK // 2, 4 * RANK), f32),
            jax.ShapeDtypeStruct((8, RANK), f32),
        ),
        in_specs=[any_spec] * 5 + [smem] * 2,
        out_specs=[vmem] * 6,
        scratch_shapes=[
            pltpu.VMEM((2 * NEAR, LEAF, LEAF), f32),
            pltpu.VMEM((2, LEAF, LEAF), f32),
            pltpu.VMEM((2, LEAF, LEAF), f32),
            pltpu.VMEM((LEAF, LEAF), f32),
            pltpu.VMEM((2, RANK, LEAF), f32),
            pltpu.VMEM((2, LEAF, LEAF), f32),
            pltpu.VMEM((2, LEAF, LEAF), f32),
            pltpu.VMEM((2, 2, LEAF, RANK), f32),
            pltpu.VMEM((9, 2, LEAF, RANK), f32),
            pltpu.VMEM((2, LEAF, RANK), f32),
            pltpu.VMEM((LEAF, RANK), f32),
            pltpu.VMEM((4, LEAF, RANK), f32),
            pltpu.VMEM((2, RANK, LEAF), f32),
            pltpu.VMEM((2, RANK, 2 * RANK), f32),
            pltpu.VMEM((2, RANK, 2 * RANK), f32),
            pltpu.VMEM((2, RANK, RANK), f32),
            pltpu.VMEM((2, 2, RANK, RANK), f32),
            pltpu.VMEM((2, RANK, 4 * RANK), f32),
            pltpu.VMEM((RANK, 4 * RANK), f32),
            pltpu.VMEM((leaves, 8, RANK), f32),
            pltpu.VMEM((groups, 8, RANK), f32),
            dma((5,)),
            dma((11,)),
            dma((12,)),
            dma((leaves,)),
            dma((leaves,)),
            dma((groups,)),
            dma((groups,)),
        ],
        compiler_params=pltpu.CompilerParams(
            collective_id=0, has_side_effects=True, vmem_limit_bytes=48 << 20
        ),
    )(near_tiles.reshape(2 * NEAR, LEAF, LEAF), diag_tiles, leaf_basis, level1_basis, level2_basis, near_index, near_mask)
    return (*outs[:5], outs[5][0, 0])


def solution(mesh):
    in_specs = (
        P(AXES, None, None, None),
        P(AXES, None, None),
        P(AXES, None),
        P(AXES, None),
        P(AXES, None, None),
        P(AXES, None, None),
        P(AXES, None),
    )
    out_specs = (
        P(AXES, None, None),
        P(AXES, None, None),
        P(AXES, None),
        P(AXES, None),
        P(AXES, None),
        P(),
    )
    return jax.shard_map(
        on_device, mesh=mesh, in_specs=in_specs, out_specs=out_specs, check_vma=False
    )
```

```python
import functools

import jax
import jax.numpy as jnp
from jax import lax
from jax.experimental import pallas as pl
from jax.experimental.pallas import tpu as pltpu
from jax.sharding import PartitionSpec as P

LEAF = 256
RANK = 128
NEAR = 16
AXES = ("grp", "leaf")
f32 = jnp.float32
bf16 = jnp.bfloat16
MESH = pl.DeviceIdType.MESH


def split(x):
    hi = x.astype(bf16)
    return hi, (x - hi.astype(f32)).astype(bf16)


def dg(a, b, ca, cb):
    return lax.dot_general(
        a, b, (((ca,), (cb,)), ((), ())), preferred_element_type=f32
    )


def dot3(a, b, ca=1, cb=0):
    ah, al = split(a)
    bh, bl = split(b)
    return dg(ah, bh, ca, cb) + (dg(ah, bl, ca, cb) + dg(al, bh, ca, cb))


def outer3(v, r):
    vh, vl = split(v)
    rh, rl = split(r)
    left = jnp.concatenate([vh, vl], axis=0)
    right = jnp.concatenate([rh, rh], axis=0)
    return dg(left, right, 0, 0) + dg(vh, rl, 0, 0)


def rowb(x, j):
    return jnp.broadcast_to(x[j : j + 1, :], x.shape)


def lane(x, i):
    return jnp.take_along_axis(x, jnp.full((8, 128), i, jnp.int32), axis=1)


def rsqrt(d):
    s = lax.rsqrt(d)
    return s * (1.5 - (0.5 * d) * (s * s))


def dot3n(a, b):
    ah, al = split(a)
    bh, bl = split(b)
    wide = dg(ah, jnp.concatenate([bh, bl], axis=1), 1, 0)
    n = b.shape[1]
    return wide[:, :n] + (wide[:, n:] + dg(al, bh, 1, 0))


def pivots(state, n):
    row = lax.broadcasted_iota(jnp.int32, (8, 128), 0)
    one = jnp.ones((8, 128), f32)
    full = [[x0, x1, cb, x0, x1, one, one] for x0, x1, cb in state]
    for j in range(8):
        for i in range(n):
            x0, x1, cb, v0, v1, d, rr = full[i]
            b = rowb(cb[j], j)
            r0 = pl.reciprocal(b, approx=True)
            e = 2.0 - b * r0
            r = r0 * e
            e = 2.0 - b * r
            here = row == j
            m = jnp.where(here, 0.0, cb[j] * r) * e
            v0 = jnp.where(here, x0, v0)
            v1 = jnp.where(here, x1, v1)
            d = jnp.where(here, b, d)
            rr = jnp.where(here, r * e, rr)
            cb = [cb[q] - m * rowb(cb[q], j) if q > j else cb[q] for q in range(8)]
            x0 = x0 - m * rowb(x0, j)
            x1 = x1 - m * rowb(x1, j)
            full[i] = [x0, x1, cb, v0, v1, d, rr]
    return full


def eliminate(A, VE, D, n):
    ahead = n == 1

    def body(k, carry):
        kk = pl.multiple_of(8 * k, 8)
        kn = pl.multiple_of(8 * jnp.minimum(k + 1, 15), 8)
        before = 8 * jnp.maximum(k - 1, 0)
        state = []
        rest = []
        for i in range(n):
            c0, c1, v0, v1, rr, p0, p1 = carry[i]
            scaled = jnp.concatenate([v0 * rr, v1 * rr], axis=1)
            if ahead:
                nxt = A[i, pl.ds(kn, 8), :]
                A[i] = A[i] - outer3(v0, scaled)
            else:
                A[i] = A[i] - outer3(v0, scaled)
                nxt = A[i, pl.ds(kn, 8), :]
            n0, n1 = nxt[:, :128], nxt[:, 128:]
            cb = [lane(c0, kk + j) for j in range(8)]
            if ahead:
                fb = [lane(n0, before + j) for j in range(8)]
                for j in range(8):
                    n0 = n0 - fb[j] * rowb(p0, j)
                    n1 = n1 - fb[j] * rowb(p1, j)
            nb = [lane(n0, kk + j) for j in range(8)]
            state.append([c0, c1, cb])
            rest.append([n0, n1, nb])
        full = pivots(state, n)
        result = []
        for i in range(n):
            x0, x1, _, v0, v1, d, rr = full[i]
            n0, n1, nb = rest[i]
            p0, p1 = x0 * rr, x1 * rr
            for j in range(8):
                n0 = n0 - nb[j] * rowb(p0, j)
                n1 = n1 - nb[j] * rowb(p1, j)
            VE[i, pl.ds(kk, 8), :] = jnp.concatenate([v0, v1], axis=1)
            D[i, pl.ds(kk, 8), :] = d
            result.append((n0, n1, v0, v1, rr, p0, p1))
        return tuple(result)

    zero = jnp.zeros((8, 128), f32)
    start = tuple((A[i, 0:8, :128], A[i, 0:8, 128:]) + (zero,) * 5 for i in range(n))
    lax.fori_loop(0, 16, body, start)


def load_system(A, i, y_rr):
    rows = lax.broadcasted_iota(jnp.int32, (RANK, RANK), 0)
    cols = lax.broadcasted_iota(jnp.int32, (RANK, RANK), 1)
    A[i, :, :RANK] = y_rr
    A[i, :, RANK:] = (rows == cols).astype(f32)


def finish(VE, D, i, y, basis_t):
    rows = lax.broadcasted_iota(jnp.int32, (RANK, RANK), 0)
    cols = lax.broadcasted_iota(jnp.int32, (RANK, RANK), 1)
    d = D[i]
    s = rsqrt(d)
    upper = jnp.where(cols >= rows, VE[i, :, :RANK] * s, 0.0)
    inverse = VE[i, :, RANK:] * s
    xh = dot3(inverse, jnp.concatenate([y[:RANK, RANK:], basis_t[:RANK]], axis=1))
    sa = jnp.concatenate([y[RANK:, RANK:], basis_t[RANK:]], axis=1) - dot3(
        xh[:, :RANK], xh, 0, 0
    )
    return upper.T, sa[:, :RANK], sa[:, RANK:]


def log_rows(d):
    return jnp.sum(jnp.log(d), axis=0, keepdims=True)


def block_system(s0, c01, c10, s1):
    return jnp.concatenate(
        [
            jnp.concatenate([s0, 0.5 * (c01 + c10.T)], axis=1),
            jnp.concatenate([0.5 * (c01.T + c10), s1], axis=1),
        ],
        axis=0,
    )


def kernel(
    groups,
    leaves,
    near,
    diag,
    leaf_basis,
    basis1,
    basis2,
    ids_hbm,
    mask_hbm,
    F0,
    F1,
    F2,
    S2,
    C2,
    LD,
    nv,
    dv,
    bv,
    b1v,
    wv,
    bt,
    yv,
    tu,
    us,
    win,
    zown,
    zsib,
    zu,
    at,
    A,
    VE,
    D,
    ex,
    pp,
    pr,
    f2,
    la,
    lg,
    ids,
    mask,
    load_sem,
    send_sem,
    recv_sem,
    la_send,
    la_recv,
    lg_send,
    lg_recv,
):
    count = groups * leaves
    g = lax.axis_index("grp")
    l = lax.axis_index("leaf")
    m = g * leaves + l
    par = lax.rem(m, 2)
    side = 2 * par - 1

    def device(k):
        return (k // leaves, lax.rem(k, leaves))

    def shifted(delta):
        return lax.rem(m + (delta + count), count)

    sibling = m - side

    loads = [
        pltpu.make_async_copy(leaf_basis, bv, load_sem.at[0]),
        pltpu.make_async_copy(basis1.at[0], b1v, load_sem.at[1]),
        pltpu.make_async_copy(basis2, wv.at[par], load_sem.at[2]),
        pltpu.make_async_copy(diag, dv, load_sem.at[3]),
        pltpu.make_async_copy(ids_hbm, ids, load_sem.at[4]),
        pltpu.make_async_copy(mask_hbm, mask, load_sem.at[5]),
        pltpu.make_async_copy(near, nv, load_sem.at[6]),
    ]
    for copy in loads[:4]:
        copy.start()

    barrier = pltpu.get_barrier_semaphore()
    direct = (-side, side, 3, -3, 4, -4)
    for delta in direct:
        pl.semaphore_signal(barrier, inc=1, device_id=device(shifted(delta)), device_id_type=MESH)

    def greet_leaf(t, _):
        pl.semaphore_signal(
            barrier, inc=1, device_id=(g, lax.rem(l + t, leaves)), device_id_type=MESH
        )
        return 0

    def greet_group(t, _):
        pl.semaphore_signal(
            barrier, inc=1, device_id=(lax.rem(g + t, groups), l), device_id_type=MESH
        )
        return 0

    lax.fori_loop(1, leaves, greet_leaf, 0)
    lax.fori_loop(1, groups, greet_group, 0)

    for copy in loads[:3]:
        copy.wait()
    for copy in loads[4:]:
        copy.start()
    q2 = wv[par, :, RANK:]
    for b in range(2):
        t = dot3(bv[b, :, RANK:], b1v[b * RANK : (b + 1) * RANK, RANK:])
        tu[1, b] = t
        tu[0, b] = dot3(t, q2)

    loads[3].wait()
    for i in range(2):
        bt[i] = bv[i].T
        y = dot3(bt[i], dot3(dv[i], bv[i]))
        yv[i] = y
        load_system(A, i, y[:RANK, :RANK])

    pl.semaphore_wait(barrier, len(direct) + (leaves - 1) + (groups - 1))

    def remote(src, dst, sent, received, target):
        return pltpu.make_async_remote_copy(
            src_ref=src,
            dst_ref=dst,
            send_sem=send_sem.at[sent],
            recv_sem=recv_sem.at[received],
            device_id=device(target),
            device_id_type=MESH,
        )

    w_send = remote(wv.at[par], wv.at[par], 6, 9, sibling)
    sends = []
    for k, delta in enumerate(direct):
        source = tu.at[1] if k == 0 else tu.at[0]
        sends.append(remote(source, win.at[4 - delta], k, 4 - delta, shifted(delta)))
    sends[0].start()
    sends[1].start()
    w_send.start()
    for copy in sends[2:]:
        copy.start()

    eliminate(A, VE, D, 2)
    for copy in loads[4:]:
        copy.wait()

    def near_block(a, j):
        slot = jnp.int32(0)
        live = f32(0.0)
        for t in range(NEAR):
            hit = jnp.logical_and(ids[a, t] == j, mask[a, t] == 1)
            slot = jnp.where(hit, t, slot)
            live = jnp.where(hit, f32(1.0), live)
        return nv[a * NEAR + slot], live

    schur = []
    logs = jnp.zeros((1, RANK), f32)
    for i in range(2):
        lower, s, a_t = finish(VE, D, i, yv[i], bt[i])
        F0[i] = lower
        at[i] = a_t
        schur.append(s)
        logs = logs + log_rows(D[i])
        tile, live = near_block(i, 2 * m + 1 - i)
        zown[i] = dot3n(tile, bv[1 - i, :, RANK:] * live)

    system = block_system(schur[0], dot3(at[0], zown[0]), dot3(at[1], zown[1]), schur[1])
    bt[0] = b1v[...].T
    y = dot3(bt[0], dot3(system, b1v[...]))
    yv[0] = y
    load_system(A, 0, y[:RANK, :RANK])

    def arrived(delta):
        slot = 4 + delta
        pltpu.make_async_copy(win.at[slot], win.at[slot], recv_sem.at[slot]).wait()

    arrived(side)
    relay_in = remote(win.at[4 + side], win.at[4 + 2 * side], 7, 4 + 2 * side, sibling)
    relay_in.start()
    eliminate(A, VE, D, 1)
    arrived(-side)

    for i in range(2):
        z = jnp.zeros((LEAF, RANK), f32)
        for c in range(2):
            tile, live = near_block(i, 2 * sibling + c)
            z = z + dot3n(tile, win[4 - side, c] * live)
        zsib[i * RANK : (i + 1) * RANK] = dot3(at[i], z)

    lower, s, a1_t = finish(VE, D, 0, yv[0], bt[0])
    F1[0] = lower
    logs = logs + log_rows(D[0])
    ex[par, 0] = s
    ex[par, 1] = dot3(a1_t, zsib[...])
    ex_send = remote(ex.at[par], ex.at[par], 9, 10, sibling)
    ex_send.start()

    w_send.wait_recv()
    q2 = wv[1 - par, :, RANK:]
    for b in range(2):
        us[b] = dot3(win[4 - side, b], q2)
    zu[...] = jnp.zeros_like(zu)
    w = jnp.concatenate([wv[0], wv[1]], axis=0)
    bt[0] = w.T
    relay_out = remote(us, win.at[4 - 2 * side], 8, 4 - 2 * side, shifted(side))
    relay_out.start()

    def far(delta):
        e = (par + delta + 8) // 2 - 4
        slot_e = jnp.where(e < 0, e + 2, e + 1)
        for a in range(2):
            z = zu[slot_e, a]
            for b in range(2):
                tile, live = near_block(a, 2 * (m + delta) + b)
                z = z + dot3n(tile, win[4 + delta, b] * live)
            zu[slot_e, a] = z

    far(side)
    arrived(4)
    far(4)

    ex_send.wait_recv()
    system = block_system(ex[0, 0], ex[0, 1], ex[1, 1], ex[1, 0])
    y = dot3(bt[0], dot3(system, w))
    yv[0] = y
    load_system(A, 0, y[:RANK, :RANK])
    eliminate(A, VE, D, 1)
    logs = logs + log_rows(D[0]) * jnp.where(par == 0, 1.0, 0.0)
    la[l] = jnp.broadcast_to(logs, (8, RANK))

    def to_leaf(t, wait):
        copy = pltpu.make_async_remote_copy(
            src_ref=la.at[l],
            dst_ref=la.at[l],
            send_sem=la_send.at[t],
            recv_sem=la_recv.at[t],
            device_id=(g, lax.rem(l + t, leaves)),
            device_id_type=MESH,
        )
        if wait:
            copy.wait()
        else:
            copy.start()

    def to_group(t, wait):
        copy = pltpu.make_async_remote_copy(
            src_ref=lg.at[g],
            dst_ref=lg.at[g],
            send_sem=lg_send.at[t],
            recv_sem=lg_recv.at[t],
            device_id=(lax.rem(g + t, groups), l),
            device_id_type=MESH,
        )
        if wait:
            copy.wait()
        else:
            copy.start()

    def each(size, step, wait):
        def body(t, _):
            step(t, wait)
            return 0

        lax.fori_loop(1, size, body, 0)

    each(leaves, to_leaf, False)
    lower, s, a2_t = finish(VE, D, 0, yv[0], bt[0])
    half = pl.multiple_of(par * (RANK // 2), RANK // 2)
    f2[:, :RANK] = lower
    f2[:, RANK:] = s
    F2[...] = f2[pl.ds(half, RANK // 2), :RANK]
    S2[...] = f2[pl.ds(half, RANK // 2), RANK:]
    chain = dot3(jnp.where(par == 0, a2_t[:, :RANK], a2_t[:, RANK:]), a1_t)
    for delta in (-4, 3, -3):
        arrived(delta)
        far(delta)
    each(leaves, to_leaf, True)
    lg[g] = jnp.sum(la[...], axis=0)
    each(groups, to_group, False)
    arrived(2 * side)
    far(2 * side)
    arrived(-2 * side)
    far(-2 * side)
    below = jnp.concatenate(
        [
            jnp.concatenate([dot3(at[a], zu[e, a]) for e in range(4)], axis=1)
            for a in range(2)
        ],
        axis=0,
    )
    part = dot3(chain, below)
    pp[0] = part[: RANK // 2]
    pp[1] = part[RANK // 2 :]
    p_send = remote(pp.at[1 - par], pr, 10, 11, sibling)
    p_send.start()
    for copy in sends:
        copy.wait_send()
    w_send.wait_send()
    ex_send.wait_send()
    relay_in.wait_send()
    relay_out.wait_send()
    p_send.wait()
    C2[...] = pp[par] + pr[...]
    each(groups, to_group, True)
    LD[...] = jnp.sum(lg[...], axis=0)


def write_out(*refs):
    sources, targets, ld, sem = refs[:5], refs[6:11], refs[11], refs[12]
    copies = [pltpu.make_async_copy(a, b, sem.at[i]) for i, (a, b) in enumerate(zip(sources, targets))]
    for copy in copies:
        copy.start()
    ld[0, 0] = refs[5][0, 0]
    for copy in copies:
        copy.wait()


def on_device(
    near_tiles, diag_tiles, near_index, near_mask, leaf_basis, level1_basis, level2_basis
):
    groups, leaves = lax.axis_size("grp"), lax.axis_size("leaf")
    hbm = pl.BlockSpec(memory_space=pltpu.HBM)
    vmem = pl.BlockSpec(memory_space=pltpu.VMEM)
    dma = pltpu.SemaphoreType.DMA
    shapes = (
        jax.ShapeDtypeStruct((2, RANK, RANK), f32),
        jax.ShapeDtypeStruct((1, RANK, RANK), f32),
        jax.ShapeDtypeStruct((RANK // 2, RANK), f32),
        jax.ShapeDtypeStruct((RANK // 2, RANK), f32),
        jax.ShapeDtypeStruct((RANK // 2, 4 * RANK), f32),
    )
    outs = pl.pallas_call(
        functools.partial(kernel, groups, leaves),
        out_shape=tuple(pltpu.VMEM(x.shape, f32) for x in shapes) + (pltpu.VMEM((8, RANK), f32),),
        in_specs=[hbm] * 7,
        out_specs=[vmem] * 6,
        scratch_shapes=[
            pltpu.VMEM((2 * NEAR, LEAF, LEAF), f32),
            pltpu.VMEM((2, LEAF, LEAF), f32),
            pltpu.VMEM((2, LEAF, LEAF), f32),
            pltpu.VMEM((LEAF, LEAF), f32),
            pltpu.VMEM((2, RANK, LEAF), f32),
            pltpu.VMEM((2, LEAF, LEAF), f32),
            pltpu.VMEM((2, LEAF, LEAF), f32),
            pltpu.VMEM((2, 2, LEAF, RANK), f32),
            pltpu.VMEM((2, LEAF, RANK), f32),
            pltpu.VMEM((9, 2, LEAF, RANK), f32),
            pltpu.VMEM((2, LEAF, RANK), f32),
            pltpu.VMEM((LEAF, RANK), f32),
            pltpu.VMEM((4, 2, LEAF, RANK), f32),
            pltpu.VMEM((2, RANK, LEAF), f32),
            pltpu.VMEM((2, RANK, 2 * RANK), f32),
            pltpu.VMEM((2, RANK, 2 * RANK), f32),
            pltpu.VMEM((2, RANK, RANK), f32),
            pltpu.VMEM((2, 2, RANK, RANK), f32),
            pltpu.VMEM((2, RANK // 2, 4 * RANK), f32),
            pltpu.VMEM((RANK // 2, 4 * RANK), f32),
            pltpu.VMEM((RANK, 2 * RANK), f32),
            pltpu.VMEM((leaves, 8, RANK), f32),
            pltpu.VMEM((groups, 8, RANK), f32),
            pltpu.SMEM((2, NEAR), jnp.int32),
            pltpu.SMEM((2, NEAR), jnp.int32),
            dma((7,)),
            dma((11,)),
            dma((12,)),
            dma((leaves,)),
            dma((leaves,)),
            dma((groups,)),
            dma((groups,)),
        ],
        compiler_params=pltpu.CompilerParams(
            collective_id=0, has_side_effects=True, vmem_limit_bytes=66000000
        ),
    )(
        near_tiles.reshape(2 * NEAR, LEAF, LEAF),
        diag_tiles,
        leaf_basis,
        level1_basis,
        level2_basis,
        near_index,
        near_mask,
    )
    outs = pl.pallas_call(
        write_out,
        out_shape=(*shapes, jax.ShapeDtypeStruct((1, 1), f32)),
        in_specs=[vmem] * 6,
        out_specs=[hbm] * 5 + [pl.BlockSpec(memory_space=pltpu.SMEM)],
        scratch_shapes=[dma((5,))],
        compiler_params=pltpu.CompilerParams(vmem_limit_bytes=1 << 20),
    )(*outs)
    return (*outs[:5], outs[5].reshape(()))


def solution(mesh):
    in_specs = (
        P(AXES, None, None, None),
        P(AXES, None, None),
        P(AXES, None),
        P(AXES, None),
        P(AXES, None, None),
        P(AXES, None, None),
        P(AXES, None),
    )
    out_specs = (
        P(AXES, None, None),
        P(AXES, None, None),
        P(AXES, None),
        P(AXES, None),
        P(AXES, None),
        P(),
    )
    return jax.shard_map(
        on_device, mesh=mesh, in_specs=in_specs, out_specs=out_specs, check_vma=False
    )
```

```python
import functools

import jax
import jax.numpy as jnp
from jax import lax
from jax.experimental import pallas as pl
from jax.experimental.pallas import tpu as pltpu
from jax.sharding import PartitionSpec as P

LEAF = 256
RANK = 128
NEAR = 16
AXES = ("grp", "leaf")
f32 = jnp.float32
bf16 = jnp.bfloat16
MESH = pl.DeviceIdType.MESH


def split(x):
    hi = x.astype(bf16)
    return hi, (x - hi.astype(f32)).astype(bf16)


def dg(a, b, ca, cb):
    return lax.dot_general(
        a, b, (((ca,), (cb,)), ((), ())), preferred_element_type=f32
    )


def dot3(a, b, ca=1, cb=0):
    ah, al = split(a)
    bh, bl = split(b)
    return dg(ah, bh, ca, cb) + (dg(ah, bl, ca, cb) + dg(al, bh, ca, cb))


def outer3(v, r):
    vh, vl = split(v)
    rh, rl = split(r)
    left = jnp.concatenate([vh, vl], axis=0)
    right = jnp.concatenate([rh, rh], axis=0)
    return dg(left, right, 0, 0) + dg(vh, rl, 0, 0)


def rowb(x, j):
    return jnp.broadcast_to(x[j : j + 1, :], x.shape)


def lane(x, i):
    return jnp.take_along_axis(x, jnp.full((8, 128), i, jnp.int32), axis=1)


def rsqrt(d):
    s = lax.rsqrt(d)
    return s * (1.5 - (0.5 * d) * (s * s))


def dot3n(a, b):
    ah, al = split(a)
    bh, bl = split(b)
    wide = dg(ah, jnp.concatenate([bh, bl], axis=1), 1, 0)
    n = b.shape[1]
    return wide[:, :n] + (wide[:, n:] + dg(al, bh, 1, 0))


def pivots(state, n):
    row = lax.broadcasted_iota(jnp.int32, (8, 128), 0)
    one = jnp.ones((8, 128), f32)
    full = [[x0, x1, cb, x0, x1, one, one] for x0, x1, cb in state]
    for j in range(8):
        for i in range(n):
            x0, x1, cb, v0, v1, d, rr = full[i]
            b = rowb(cb[j], j)
            r0 = pl.reciprocal(b, approx=True)
            e = 2.0 - b * r0
            r = r0 * e
            e = 2.0 - b * r
            here = row == j
            m = jnp.where(here, 0.0, cb[j] * r) * e
            v0 = jnp.where(here, x0, v0)
            v1 = jnp.where(here, x1, v1)
            d = jnp.where(here, b, d)
            rr = jnp.where(here, r * e, rr)
            cb = [cb[q] - m * rowb(cb[q], j) if q > j else cb[q] for q in range(8)]
            x0 = x0 - m * rowb(x0, j)
            x1 = x1 - m * rowb(x1, j)
            full[i] = [x0, x1, cb, v0, v1, d, rr]
    return full


def eliminate(A, VE, D, n):
    ahead = n == 1

    def body(k, carry):
        kk = pl.multiple_of(8 * k, 8)
        kn = pl.multiple_of(8 * jnp.minimum(k + 1, 15), 8)
        before = 8 * jnp.maximum(k - 1, 0)
        state = []
        rest = []
        for i in range(n):
            c0, c1, v0, v1, rr, p0, p1 = carry[i]
            scaled = jnp.concatenate([v0 * rr, v1 * rr], axis=1)
            if ahead:
                nxt = A[i, pl.ds(kn, 8), :]
                A[i] = A[i] - outer3(v0, scaled)
            else:
                A[i] = A[i] - outer3(v0, scaled)
                nxt = A[i, pl.ds(kn, 8), :]
            n0, n1 = nxt[:, :128], nxt[:, 128:]
            cb = [lane(c0, kk + j) for j in range(8)]
            if ahead:
                fb = [lane(n0, before + j) for j in range(8)]
                for j in range(8):
                    n0 = n0 - fb[j] * rowb(p0, j)
                    n1 = n1 - fb[j] * rowb(p1, j)
            nb = [lane(n0, kk + j) for j in range(8)]
            state.append([c0, c1, cb])
            rest.append([n0, n1, nb])
        full = pivots(state, n)
        result = []
        for i in range(n):
            x0, x1, _, v0, v1, d, rr = full[i]
            n0, n1, nb = rest[i]
            p0, p1 = x0 * rr, x1 * rr
            for j in range(8):
                n0 = n0 - nb[j] * rowb(p0, j)
                n1 = n1 - nb[j] * rowb(p1, j)
            VE[i, pl.ds(kk, 8), :] = jnp.concatenate([v0, v1], axis=1)
            D[i, pl.ds(kk, 8), :] = d
            result.append((n0, n1, v0, v1, rr, p0, p1))
        return tuple(result)

    zero = jnp.zeros((8, 128), f32)
    start = tuple((A[i, 0:8, :128], A[i, 0:8, 128:]) + (zero,) * 5 for i in range(n))
    lax.fori_loop(0, 16, body, start)


def load_system(A, i, y_rr):
    rows = lax.broadcasted_iota(jnp.int32, (RANK, RANK), 0)
    cols = lax.broadcasted_iota(jnp.int32, (RANK, RANK), 1)
    A[i, :, :RANK] = y_rr
    A[i, :, RANK:] = (rows == cols).astype(f32)


def lower_factor(VE, D, i):
    rows = lax.broadcasted_iota(jnp.int32, (RANK, RANK), 0)
    cols = lax.broadcasted_iota(jnp.int32, (RANK, RANK), 1)
    return jnp.where(cols >= rows, VE[i, :, :RANK] * rsqrt(D[i]), 0.0).T


def reduced(VE, D, i, y, basis_t):
    inverse = VE[i, :, RANK:] * rsqrt(D[i])
    xh = dot3(inverse, jnp.concatenate([y[:RANK, RANK:], basis_t[:RANK]], axis=1))
    sa = jnp.concatenate([y[RANK:, RANK:], basis_t[RANK:]], axis=1) - dot3(
        xh[:, :RANK], xh, 0, 0
    )
    return sa[:, :RANK], sa[:, RANK:]


def log_rows(d):
    return jnp.sum(jnp.log(d), axis=0, keepdims=True)


def block_system(s0, c01, c10, s1):
    return jnp.concatenate(
        [
            jnp.concatenate([s0, 0.5 * (c01 + c10.T)], axis=1),
            jnp.concatenate([0.5 * (c01.T + c10), s1], axis=1),
        ],
        axis=0,
    )


def kernel(
    groups,
    leaves,
    near,
    diag,
    leaf_basis,
    basis1,
    basis2,
    ids_hbm,
    mask_hbm,
    F0,
    F1,
    F2,
    S2,
    C2,
    LD,
    nv,
    dv,
    bv,
    b1v,
    wv,
    bt,
    yv,
    tu,
    us,
    win,
    zown,
    zsib,
    zu,
    at,
    A,
    VE,
    D,
    ex,
    pp,
    pr,
    f2,
    la,
    lg,
    ids,
    mask,
    load_sem,
    send_sem,
    recv_sem,
    la_send,
    la_recv,
    lg_send,
    lg_recv,
):
    count = groups * leaves
    g = lax.axis_index("grp")
    l = lax.axis_index("leaf")
    m = g * leaves + l
    par = lax.rem(m, 2)
    side = 2 * par - 1

    def device(k):
        return (k // leaves, lax.rem(k, leaves))

    def shifted(delta):
        return lax.rem(m + (delta + count), count)

    sibling = m - side

    loads = [
        pltpu.make_async_copy(leaf_basis, bv, load_sem.at[0]),
        pltpu.make_async_copy(basis1.at[0], b1v, load_sem.at[1]),
        pltpu.make_async_copy(basis2, wv.at[par], load_sem.at[2]),
        pltpu.make_async_copy(diag, dv, load_sem.at[3]),
        pltpu.make_async_copy(ids_hbm, ids, load_sem.at[4]),
        pltpu.make_async_copy(mask_hbm, mask, load_sem.at[5]),
        pltpu.make_async_copy(near, nv, load_sem.at[6]),
    ]
    for copy in loads[:4]:
        copy.start()

    barrier = pltpu.get_barrier_semaphore()
    direct = (-side, side, 4, -4)
    for delta in direct:
        pl.semaphore_signal(barrier, inc=1, device_id=device(shifted(delta)), device_id_type=MESH)

    def greet_leaf(t, _):
        pl.semaphore_signal(
            barrier, inc=1, device_id=(g, lax.rem(l + t, leaves)), device_id_type=MESH
        )
        return 0

    def greet_group(t, _):
        pl.semaphore_signal(
            barrier, inc=1, device_id=(lax.rem(g + t, groups), l), device_id_type=MESH
        )
        return 0

    lax.fori_loop(1, leaves, greet_leaf, 0)
    lax.fori_loop(1, groups, greet_group, 0)

    for copy in loads[:3]:
        copy.wait()
    for copy in loads[4:]:
        copy.start()
    q2 = wv[par, :, RANK:]
    for b in range(2):
        t = dot3(bv[b, :, RANK:], b1v[b * RANK : (b + 1) * RANK, RANK:])
        tu[1, b] = t
        tu[0, b] = dot3(t, q2)

    loads[3].wait()
    for i in range(2):
        bt[i] = bv[i].T
        y = dot3(bt[i], dot3(dv[i], bv[i]))
        yv[i] = y
        load_system(A, i, y[:RANK, :RANK])

    pl.semaphore_wait(barrier, len(direct) + (leaves - 1) + (groups - 1))

    def remote(src, dst, sent, received, target):
        return pltpu.make_async_remote_copy(
            src_ref=src,
            dst_ref=dst,
            send_sem=send_sem.at[sent],
            recv_sem=recv_sem.at[received],
            device_id=device(target),
            device_id_type=MESH,
        )

    w_send = remote(wv.at[par], wv.at[par], 6, 9, sibling)
    sends = []
    for k, delta in enumerate(direct):
        source = tu.at[1] if k == 0 else tu.at[0]
        sends.append(remote(source, win.at[4 - delta], k, 4 - delta, shifted(delta)))
    sends[0].start()
    sends[1].start()
    w_send.start()
    for copy in sends[2:]:
        copy.start()

    eliminate(A, VE, D, 2)
    for copy in loads[4:]:
        copy.wait()

    def near_block(a, j):
        slot = jnp.int32(0)
        live = f32(0.0)
        for t in range(NEAR):
            hit = jnp.logical_and(ids[a, t] == j, mask[a, t] == 1)
            slot = jnp.where(hit, t, slot)
            live = jnp.where(hit, f32(1.0), live)
        return nv[a * NEAR + slot], live

    schur = []
    logs = jnp.zeros((1, RANK), f32)
    for i in range(2):
        s, a_t = reduced(VE, D, i, yv[i], bt[i])
        F0[i] = lower_factor(VE, D, i)
        at[i] = a_t
        schur.append(s)
        logs = logs + log_rows(D[i])
        tile, live = near_block(i, 2 * m + 1 - i)
        zown[i] = dot3n(tile, bv[1 - i, :, RANK:] * live)

    system = block_system(schur[0], dot3(at[0], zown[0]), dot3(at[1], zown[1]), schur[1])
    bt[0] = b1v[...].T
    y = dot3(bt[0], dot3(system, b1v[...]))
    yv[0] = y
    load_system(A, 0, y[:RANK, :RANK])

    def arrived(delta):
        slot = 4 + delta
        pltpu.make_async_copy(win.at[slot], win.at[slot], recv_sem.at[slot]).wait()

    eliminate(A, VE, D, 1)
    arrived(-side)

    for i in range(2):
        z = jnp.zeros((LEAF, RANK), f32)
        for c in range(2):
            tile, live = near_block(i, 2 * sibling + c)
            z = z + dot3n(tile, win[4 - side, c] * live)
        zsib[i * RANK : (i + 1) * RANK] = dot3(at[i], z)

    s, a1_t = reduced(VE, D, 0, yv[0], bt[0])
    ex[par, 0] = s
    ex[par, 1] = dot3(a1_t, zsib[...])
    ex_send = remote(ex.at[par], ex.at[par], 9, 10, sibling)
    ex_send.start()
    F1[0] = lower_factor(VE, D, 0)
    logs = logs + log_rows(D[0])
    arrived(side)
    relays = [
        remote(win.at[4 + side], win.at[4 - 3 * side], 4, 4 - 3 * side, shifted(4 * side)),
        remote(us, win.at[4 + 3 * side], 5, 4 + 3 * side, shifted(-4 * side)),
        remote(us, win.at[4 - 2 * side], 8, 4 - 2 * side, shifted(side)),
        remote(win.at[4 + side], win.at[4 + 2 * side], 7, 4 + 2 * side, sibling),
    ]
    relays[0].start()

    w_send.wait_recv()
    q2 = wv[1 - par, :, RANK:]
    for b in range(2):
        us[b] = dot3(win[4 - side, b], q2)
    relays[1].start()
    relays[2].start()
    zu[...] = jnp.zeros_like(zu)
    w = jnp.concatenate([wv[0], wv[1]], axis=0)
    bt[0] = w.T

    def far(delta):
        e = (par + delta + 8) // 2 - 4
        slot_e = jnp.where(e < 0, e + 2, e + 1)
        for a in range(2):
            z = zu[slot_e, a]
            for b in range(2):
                tile, live = near_block(a, 2 * (m + delta) + b)
                z = z + dot3n(tile, win[4 + delta, b] * live)
            zu[slot_e, a] = z

    far(side)
    arrived(4)
    arrived(-4)
    far(4)
    far(-4)

    ex_send.wait_recv()
    relays[3].start()
    system = block_system(ex[0, 0], ex[0, 1], ex[1, 1], ex[1, 0])
    y = dot3(bt[0], dot3(system, w))
    yv[0] = y
    load_system(A, 0, y[:RANK, :RANK])
    eliminate(A, VE, D, 1)
    logs = logs + log_rows(D[0]) * jnp.where(par == 0, 1.0, 0.0)
    la[l] = logs

    def to_leaf(t, wait):
        copy = pltpu.make_async_remote_copy(
            src_ref=la.at[l],
            dst_ref=la.at[l],
            send_sem=la_send.at[t],
            recv_sem=la_recv.at[t],
            device_id=(g, lax.rem(l + t, leaves)),
            device_id_type=MESH,
        )
        if wait:
            copy.wait()
        else:
            copy.start()

    def to_group(t, wait):
        copy = pltpu.make_async_remote_copy(
            src_ref=lg.at[g],
            dst_ref=lg.at[g],
            send_sem=lg_send.at[t],
            recv_sem=lg_recv.at[t],
            device_id=(lax.rem(g + t, groups), l),
            device_id_type=MESH,
        )
        if wait:
            copy.wait()
        else:
            copy.start()

    def each(size, step, wait):
        def body(t, _):
            step(t, wait)
            return 0

        lax.fori_loop(1, size, body, 0)

    each(leaves, to_leaf, False)
    s, a2_t = reduced(VE, D, 0, yv[0], bt[0])
    half = pl.multiple_of(par * (RANK // 2), RANK // 2)
    f2[:, :RANK] = lower_factor(VE, D, 0)
    f2[:, RANK:] = s
    F2[...] = f2[pl.ds(half, RANK // 2), :RANK]
    S2[...] = f2[pl.ds(half, RANK // 2), RANK:]
    chain = dot3(jnp.where(par == 0, a2_t[:, :RANK], a2_t[:, RANK:]), a1_t)
    for delta in (-3 * side, 3 * side):
        arrived(delta)
        far(delta)
    each(leaves, to_leaf, True)
    lg[g] = jnp.sum(la[...], axis=0)
    each(groups, to_group, False)
    arrived(-2 * side)
    far(-2 * side)
    arrived(2 * side)
    far(2 * side)
    below = jnp.concatenate(
        [
            jnp.concatenate([dot3(at[a], zu[e, a]) for e in range(4)], axis=1)
            for a in range(2)
        ],
        axis=0,
    )
    part = dot3(chain, below)
    pp[0] = part[: RANK // 2]
    pp[1] = part[RANK // 2 :]
    p_send = remote(pp.at[1 - par], pr, 10, 11, sibling)
    p_send.start()
    for copy in sends:
        copy.wait_send()
    w_send.wait_send()
    ex_send.wait_send()
    for copy in relays:
        copy.wait_send()
    p_send.wait()
    C2[...] = pp[par] + pr[...]
    each(groups, to_group, True)
    LD[...] = jnp.sum(lg[...], axis=0)


def write_out(*refs):
    sources, targets, ld, sem = refs[:5], refs[6:11], refs[11], refs[12]
    copies = [pltpu.make_async_copy(a, b, sem.at[i]) for i, (a, b) in enumerate(zip(sources, targets))]
    for copy in copies:
        copy.start()
    ld[0, 0] = refs[5][0, 0]
    for copy in copies:
        copy.wait()


def on_device(
    near_tiles, diag_tiles, near_index, near_mask, leaf_basis, level1_basis, level2_basis
):
    groups, leaves = lax.axis_size("grp"), lax.axis_size("leaf")
    hbm = pl.BlockSpec(memory_space=pltpu.HBM)
    vmem = pl.BlockSpec(memory_space=pltpu.VMEM)
    dma = pltpu.SemaphoreType.DMA
    shapes = (
        jax.ShapeDtypeStruct((2, RANK, RANK), f32),
        jax.ShapeDtypeStruct((1, RANK, RANK), f32),
        jax.ShapeDtypeStruct((RANK // 2, RANK), f32),
        jax.ShapeDtypeStruct((RANK // 2, RANK), f32),
        jax.ShapeDtypeStruct((RANK // 2, 4 * RANK), f32),
    )
    outs = pl.pallas_call(
        functools.partial(kernel, groups, leaves),
        out_shape=tuple(pltpu.VMEM(x.shape, f32) for x in shapes) + (pltpu.VMEM((1, RANK), f32),),
        in_specs=[hbm] * 7,
        out_specs=[vmem] * 6,
        scratch_shapes=[
            pltpu.VMEM((2 * NEAR, LEAF, LEAF), f32),
            pltpu.VMEM((2, LEAF, LEAF), f32),
            pltpu.VMEM((2, LEAF, LEAF), f32),
            pltpu.VMEM((LEAF, LEAF), f32),
            pltpu.VMEM((2, RANK, LEAF), f32),
            pltpu.VMEM((2, LEAF, LEAF), f32),
            pltpu.VMEM((2, LEAF, LEAF), f32),
            pltpu.VMEM((2, 2, LEAF, RANK), f32),
            pltpu.VMEM((2, LEAF, RANK), f32),
            pltpu.VMEM((9, 2, LEAF, RANK), f32),
            pltpu.VMEM((2, LEAF, RANK), f32),
            pltpu.VMEM((LEAF, RANK), f32),
            pltpu.VMEM((4, 2, LEAF, RANK), f32),
            pltpu.VMEM((2, RANK, LEAF), f32),
            pltpu.VMEM((2, RANK, 2 * RANK), f32),
            pltpu.VMEM((2, RANK, 2 * RANK), f32),
            pltpu.VMEM((2, RANK, RANK), f32),
            pltpu.VMEM((2, 2, RANK, RANK), f32),
            pltpu.VMEM((2, RANK // 2, 4 * RANK), f32),
            pltpu.VMEM((RANK // 2, 4 * RANK), f32),
            pltpu.VMEM((RANK, 2 * RANK), f32),
            pltpu.VMEM((leaves, 1, RANK), f32),
            pltpu.VMEM((groups, 1, RANK), f32),
            pltpu.SMEM((2, NEAR), jnp.int32),
            pltpu.SMEM((2, NEAR), jnp.int32),
            dma((7,)),
            dma((11,)),
            dma((12,)),
            dma((leaves,)),
            dma((leaves,)),
            dma((groups,)),
            dma((groups,)),
        ],
        compiler_params=pltpu.CompilerParams(
            collective_id=0, has_side_effects=True, vmem_limit_bytes=66000000
        ),
    )(
        near_tiles.reshape(2 * NEAR, LEAF, LEAF),
        diag_tiles,
        leaf_basis,
        level1_basis,
        level2_basis,
        near_index,
        near_mask,
    )
    outs = pl.pallas_call(
        write_out,
        out_shape=(*shapes, jax.ShapeDtypeStruct((1, 1), f32)),
        in_specs=[vmem] * 6,
        out_specs=[hbm] * 5 + [pl.BlockSpec(memory_space=pltpu.SMEM)],
        scratch_shapes=[dma((5,))],
        compiler_params=pltpu.CompilerParams(vmem_limit_bytes=1 << 20),
    )(*outs)
    return (*outs[:5], outs[5].reshape(()))


def solution(mesh):
    in_specs = (
        P(AXES, None, None, None),
        P(AXES, None, None),
        P(AXES, None),
        P(AXES, None),
        P(AXES, None, None),
        P(AXES, None, None),
        P(AXES, None),
    )
    out_specs = (
        P(AXES, None, None),
        P(AXES, None, None),
        P(AXES, None),
        P(AXES, None),
        P(AXES, None),
        P(),
    )
    return jax.shard_map(
        on_device, mesh=mesh, in_specs=in_specs, out_specs=out_specs, check_vma=False
    )
```

```python
import functools

import jax
import jax.numpy as jnp
from jax import lax
from jax.experimental import pallas as pl
from jax.experimental.pallas import tpu as pltpu
from jax.sharding import PartitionSpec as P

LEAF = 256
RANK = 128
NEAR = 16
AXES = ("grp", "leaf")
f32 = jnp.float32
bf16 = jnp.bfloat16
MESH = pl.DeviceIdType.MESH


def split(x):
    hi = x.astype(bf16)
    return hi, (x - hi.astype(f32)).astype(bf16)


def dg(a, b, ca, cb):
    return lax.dot_general(
        a, b, (((ca,), (cb,)), ((), ())), preferred_element_type=f32
    )


def dot3(a, b, ca=1, cb=0):
    ah, al = split(a)
    bh, bl = split(b)
    return dg(ah, bh, ca, cb) + (dg(ah, bl, ca, cb) + dg(al, bh, ca, cb))


def rowb(x, j):
    return jnp.broadcast_to(x[j : j + 1, :], x.shape)


def lane(x, i):
    return jnp.take_along_axis(x, jnp.full((8, 128), i, jnp.int32), axis=1)


def rsqrt(d):
    s = lax.rsqrt(d)
    return s * (1.5 - (0.5 * d) * (s * s))


def halves(b):
    bh, bl = split(b)
    return jnp.concatenate([bh, bl], axis=1)


def dot3n(a, wide):
    ah, al = split(a)
    n = wide.shape[1] // 2
    both = dg(ah, wide, 1, 0)
    return both[:, :n] + (both[:, n:] + dg(al, wide[:, :n], 1, 0))


def eliminate(A, E, D, Zh, Zl, n, base):
    ahead = n == 1
    row = lax.broadcasted_iota(jnp.int32, (8, 128), 0)
    col = lax.broadcasted_iota(jnp.int32, (8, 128), 1)

    def body(k, carry):
        kk = pl.multiple_of(8 * k, 8)
        kn = pl.multiple_of(8 * jnp.minimum(k + 1, 15), 8)
        before = 8 * jnp.maximum(k - 1, 0)
        now = jnp.logical_and(col >= kk, col < kk + 8)
        last = jnp.logical_and(col >= kk - 8, col < kk)
        last_all = jnp.broadcast_to(last[0:1, :], (RANK, RANK))
        unit = (col == row + kk).astype(f32)
        state = []
        for i in range(n):
            c, p = carry[i]
            if ahead:
                nxt = A[i, pl.ds(kn, 8), :]
            whole = A[i]
            hi, lo = split(whole)
            zh, zl = Zh[i], Zl[i]
            update = dg(hi, zh, 1, 0) + (dg(hi, zl, 1, 0) + dg(lo, zh, 1, 0))
            A[i] = jnp.where(last_all, 0.0, whole) - update
            if not ahead:
                nxt = A[i, pl.ds(kn, 8), :]
            cb = [lane(c, kk + j) for j in range(8)]
            if ahead:
                fb = [lane(nxt, before + j) for j in range(8)]
                nxt = jnp.where(last, 0.0, nxt)
                for j in range(8):
                    nxt = nxt - fb[j] * rowb(p, j)
            nb = [lane(nxt, kk + j) for j in range(8)]
            nxt = jnp.where(now, 0.0, nxt)
            x = jnp.where(now, unit, c)
            one = jnp.ones_like(c)
            state.append([x, nxt, cb, nb, x, one, one])
        for j in range(8):
            for i in range(n):
                x, nxt, cb, nb, v, d, rr = state[i]
                b = rowb(cb[j], j)
                r = pl.reciprocal(b, approx=True)
                e = 2.0 - b * r
                here = row == j
                m = jnp.where(here, 0.0, cb[j] * r) * e
                v = jnp.where(here, x, v)
                d = jnp.where(here, b, d)
                rr = jnp.where(here, r * e, rr)
                cb = [cb[q] - m * rowb(cb[q], j) if q > j else cb[q] for q in range(8)]
                x = x - m * rowb(x, j)
                state[i] = [x, nxt, cb, nb, v, d, rr]
        even = lax.rem(k, 2) == 0
        pair = pl.multiple_of(16 * (k // 2), 16)
        old = pl.multiple_of(16 * (jnp.maximum(k - 1, 0) // 2), 16)
        result = []
        for i in range(n):
            x, nxt, cb, nb, v, d, rr = state[i]
            p = x * rr
            for j in range(8):
                nxt = nxt - nb[j] * rowb(p, j)
            E[base + i, pl.ds(kk, 8), :] = v
            D[base + i, pl.ds(kk, 8), :] = d
            none = jnp.zeros((16, RANK), bf16)
            Zh[i, pl.ds(old, 16), :] = none
            Zl[i, pl.ds(old, 16), :] = none
            hi, lo = split(
                jnp.concatenate([jnp.where(even, p, 0.0), jnp.where(even, 0.0, p)], axis=0)
            )
            Zh[i, pl.ds(pair, 16), :] = hi
            Zl[i, pl.ds(pair, 16), :] = lo
            result.append((nxt, p))
        return tuple(result)

    Zh[...] = jnp.zeros_like(Zh)
    Zl[...] = jnp.zeros_like(Zl)
    zero = jnp.zeros((8, RANK), f32)
    lax.fori_loop(0, 16, body, tuple((A[i, 0:8, :], zero) for i in range(n)))


def lower_mask():
    rows = lax.broadcasted_iota(jnp.int32, (RANK, RANK), 0)
    cols = lax.broadcasted_iota(jnp.int32, (RANK, RANK), 1)
    return cols <= rows


def lower_factor(E, y, i):
    product = lax.dot_general(
        y[i, :RANK, :RANK],
        E[i],
        (((1,), (1,)), ((), ())),
        precision=lax.Precision.HIGHEST,
        preferred_element_type=f32,
    )
    return jnp.where(lower_mask(), product, 0.0)


def reduced(E, D, y, i, basis_t):
    inverse = jnp.where(lower_mask(), E[i] * rsqrt(D[i]), 0.0)
    E[i] = inverse
    xh = dot3(
        inverse, jnp.concatenate([y[i, :RANK, RANK:], basis_t[:RANK]], axis=1)
    )
    sa = jnp.concatenate([y[i, RANK:, RANK:], basis_t[RANK:]], axis=1) - dot3(
        xh[:, :RANK], xh, 0, 0
    )
    return sa[:, :RANK], sa[:, RANK:]


def log_rows(d):
    return jnp.sum(jnp.log(d), axis=0, keepdims=True)


def block_system(s0, c01, c10, s1):
    return jnp.concatenate(
        [
            jnp.concatenate([s0, 0.5 * (c01 + c10.T)], axis=1),
            jnp.concatenate([0.5 * (c01.T + c10), s1], axis=1),
        ],
        axis=0,
    )


def kernel(
    groups,
    leaves,
    near,
    diag,
    leaf_basis,
    basis1,
    basis2,
    ids_hbm,
    mask_hbm,
    F0,
    F1,
    F2,
    S2,
    C2,
    LD,
    nv,
    dv,
    bv,
    b1v,
    wv,
    bt,
    yv,
    tu,
    us,
    win,
    zown,
    zsib,
    zu,
    at,
    A,
    E,
    D,
    Zh,
    Zl,
    ex,
    pp,
    pr,
    f2,
    la,
    lg,
    ids,
    mask,
    load_sem,
    send_sem,
    recv_sem,
    la_send,
    la_recv,
    lg_send,
    lg_recv,
    part_send,
    part_recv,
):
    count = groups * leaves
    g = lax.axis_index("grp")
    l = lax.axis_index("leaf")
    m = g * leaves + l
    par = lax.rem(m, 2)
    side = 2 * par - 1

    def device(k):
        return (k // leaves, lax.rem(k, leaves))

    def shifted(delta):
        return lax.rem(m + (delta + count), count)

    sibling = m - side

    loads = [
        pltpu.make_async_copy(leaf_basis, bv, load_sem.at[0]),
        pltpu.make_async_copy(basis1.at[0], b1v, load_sem.at[1]),
        pltpu.make_async_copy(basis2, wv.at[par], load_sem.at[2]),
        pltpu.make_async_copy(diag, dv, load_sem.at[3]),
        pltpu.make_async_copy(ids_hbm, ids, load_sem.at[4]),
        pltpu.make_async_copy(mask_hbm, mask, load_sem.at[5]),
        pltpu.make_async_copy(near, nv, load_sem.at[6]),
    ]
    for copy in loads[:3]:
        copy.start()

    barrier = pltpu.get_barrier_semaphore()
    direct = (-side, side, 4, -4)
    for delta in direct:
        pl.semaphore_signal(barrier, inc=1, device_id=device(shifted(delta)), device_id_type=MESH)

    def greet_leaf(t, _):
        pl.semaphore_signal(
            barrier, inc=1, device_id=(g, lax.rem(l + t, leaves)), device_id_type=MESH
        )
        return 0

    def greet_group(t, _):
        pl.semaphore_signal(
            barrier, inc=1, device_id=(lax.rem(g + t, groups), l), device_id_type=MESH
        )
        return 0

    lax.fori_loop(1, leaves, greet_leaf, 0)
    lax.fori_loop(1, groups, greet_group, 0)
    loads[3].start()

    for copy in loads[:3]:
        copy.wait()
    for copy in loads[4:]:
        copy.start()
    q2 = wv[par, :, RANK:]
    for b in range(2):
        t = dot3(bv[b, :, RANK:], b1v[b * RANK : (b + 1) * RANK, RANK:])
        tu[1, b] = t
        tu[0, b] = dot3(t, q2)

    loads[3].wait()
    for i in range(2):
        bt[i] = bv[i].T
        y = dot3(bt[i], dot3(dv[i], bv[i]))
        yv[i] = y
        A[i] = y[:RANK, :RANK]
    bt[2] = b1v[...].T

    pl.semaphore_wait(barrier, len(direct) + (leaves - 1) + (groups - 1))

    def remote(src, dst, sent, received, target):
        return pltpu.make_async_remote_copy(
            src_ref=src,
            dst_ref=dst,
            send_sem=send_sem.at[sent],
            recv_sem=recv_sem.at[received],
            device_id=device(target),
            device_id_type=MESH,
        )

    w_send = remote(wv.at[par], wv.at[par], 6, 9, sibling)
    sends = []
    for k, delta in enumerate(direct):
        source = tu.at[1] if k == 0 else tu.at[0]
        sends.append(remote(source, win.at[4 - delta], k, 4 - delta, shifted(delta)))
    sends[0].start()
    sends[1].start()
    w_send.start()
    for copy in sends[2:]:
        copy.start()

    eliminate(A, E, D, Zh, Zl, 2, 0)
    for copy in loads[4:]:
        copy.wait()

    def near_block(a, j):
        slot = jnp.int32(0)
        live = f32(0.0)
        for t in range(NEAR):
            hit = jnp.logical_and(ids[a, t] == j, mask[a, t] == 1)
            slot = jnp.where(hit, t, slot)
            live = jnp.where(hit, f32(1.0), live)
        return nv[a * NEAR + slot], live

    schur = []
    for i in range(2):
        s, a_t = reduced(E, D, yv, i, bt[i])
        at[i] = a_t
        schur.append(s)
        tile, live = near_block(i, 2 * m + 1 - i)
        zown[i] = dot3n(tile, halves(bv[1 - i, :, RANK:])) * live

    system = block_system(schur[0], dot3(at[0], zown[0]), dot3(at[1], zown[1]), schur[1])
    y = dot3(bt[2], dot3(system, b1v[...]))
    yv[2] = y
    A[0] = y[:RANK, :RANK]

    def arrived(delta):
        slot = 4 + delta
        pltpu.make_async_copy(win.at[slot], win.at[slot], recv_sem.at[slot]).wait()

    eliminate(A, E, D, Zh, Zl, 1, 2)
    arrived(-side)

    right = [halves(win[4 - side, c]) for c in range(2)]
    for i in range(2):
        z = jnp.zeros((LEAF, RANK), f32)
        for c in range(2):
            tile, live = near_block(i, 2 * sibling + c)
            z = z + dot3n(tile, right[c]) * live
        zsib[i * RANK : (i + 1) * RANK] = dot3(at[i], z)

    s, a1_t = reduced(E, D, yv, 2, bt[2])
    ex[par, 0] = s
    ex_sends = [remote(ex.at[par, i], ex.at[par, i], 9 + 2 * i, 10 + 2 * i, sibling) for i in range(2)]
    ex_sends[0].start()
    ex[par, 1] = dot3(a1_t, zsib[...])
    ex_sends[1].start()
    arrived(side)
    relays = [
        remote(win.at[4 + side], win.at[4 - 3 * side], 4, 4 - 3 * side, shifted(4 * side)),
        remote(us, win.at[4 + 3 * side], 5, 4 + 3 * side, shifted(-4 * side)),
        remote(us, win.at[4 - 2 * side], 8, 4 - 2 * side, shifted(side)),
        remote(win.at[4 + side], win.at[4 + 2 * side], 7, 4 + 2 * side, sibling),
    ]
    relays[0].start()

    w_send.wait_recv()
    q2 = wv[1 - par, :, RANK:]
    for b in range(2):
        us[b] = dot3(win[4 - side, b], q2)
    relays[1].start()
    zu[...] = jnp.zeros_like(zu)
    w = jnp.concatenate([wv[0], wv[1]], axis=0)
    bt[3] = w.T

    def far(delta):
        e = (par + delta + 8) // 2 - 4
        slot_e = jnp.where(e < 0, e + 2, e + 1)
        right = [halves(win[4 + delta, b]) for b in range(2)]
        for a in range(2):
            z = zu[slot_e, a]
            for b in range(2):
                tile, live = near_block(a, 2 * (m + delta) + b)
                z = z + dot3n(tile, right[b]) * live
            zu[slot_e, a] = z

    far(side)
    arrived(4)
    arrived(-4)
    far(4)
    far(-4)

    for i in range(2):
        F0[i] = lower_factor(E, yv, i)
    F1[0] = lower_factor(E, yv, 2)
    logs = log_rows(D[0]) + log_rows(D[1]) + log_rows(D[2])

    for copy in ex_sends:
        copy.wait_recv()
    relays[2].start()
    relays[3].start()
    system = block_system(ex[0, 0], ex[0, 1], ex[1, 1], ex[1, 0])
    y = dot3(bt[3], dot3(system, w))
    yv[3] = y
    A[0] = y[:RANK, :RANK]
    eliminate(A, E, D, Zh, Zl, 1, 3)
    logs = logs + log_rows(D[3]) * jnp.where(par == 0, 1.0, 0.0)
    la[l] = logs

    def to_leaf(t, wait):
        copy = pltpu.make_async_remote_copy(
            src_ref=la.at[l],
            dst_ref=la.at[l],
            send_sem=la_send.at[t],
            recv_sem=la_recv.at[t],
            device_id=(g, lax.rem(l + t, leaves)),
            device_id_type=MESH,
        )
        if wait:
            copy.wait()
        else:
            copy.start()

    def to_group(t, wait):
        copy = pltpu.make_async_remote_copy(
            src_ref=lg.at[g],
            dst_ref=lg.at[g],
            send_sem=lg_send.at[t],
            recv_sem=lg_recv.at[t],
            device_id=(lax.rem(g + t, groups), l),
            device_id_type=MESH,
        )
        if wait:
            copy.wait()
        else:
            copy.start()

    def each(size, step, wait):
        def body(t, _):
            step(t, wait)
            return 0

        lax.fori_loop(1, size, body, 0)

    each(leaves, to_leaf, False)
    s, a2_t = reduced(E, D, yv, 3, bt[3])
    half = pl.multiple_of(par * (RANK // 2), RANK // 2)
    f2[:, :RANK] = lower_factor(E, yv, 3)
    f2[:, RANK:] = s
    F2[...] = f2[pl.ds(half, RANK // 2), :RANK]
    S2[...] = f2[pl.ds(half, RANK // 2), RANK:]
    chain = dot3(jnp.where(par == 0, a2_t[:, :RANK], a2_t[:, RANK:]), a1_t)

    def reduce_part(e):
        i = jnp.where(e < 0, e + 2, e + 1)
        below = jnp.concatenate([dot3(at[a], zu[i, a]) for a in range(2)], axis=0)
        part = dot3(chain, below)
        pp[0, i] = part[: RANK // 2]
        pp[1, i] = part[RANK // 2 :]
        copy = pltpu.make_async_remote_copy(
            src_ref=pp.at[1 - par, i],
            dst_ref=pr.at[i],
            send_sem=part_send.at[i],
            recv_sem=part_recv.at[i],
            device_id=device(sibling),
            device_id_type=MESH,
        )
        copy.start()
        return copy

    parts = [reduce_part(-2 * side)]
    arrived(-3 * side)
    far(-3 * side)
    arrived(-2 * side)
    far(-2 * side)
    parts.append(reduce_part(-side))
    each(leaves, to_leaf, True)
    lg[g] = jnp.sum(la[...], axis=0)
    each(groups, to_group, False)
    arrived(3 * side)
    far(3 * side)
    parts.append(reduce_part(2 * side))
    arrived(2 * side)
    far(2 * side)
    parts.append(reduce_part(side))
    for copy in sends:
        copy.wait_send()
    w_send.wait_send()
    for copy in ex_sends:
        copy.wait_send()
    for copy in relays:
        copy.wait_send()
    for copy in parts:
        copy.wait()
    for i in range(4):
        C2[:, i * RANK : (i + 1) * RANK] = pp[par, i] + pr[i]
    each(groups, to_group, True)
    LD[...] = jnp.sum(lg[...], axis=0)


def write_out(*refs):
    sources, targets, ld, sem = refs[:5], refs[6:11], refs[11], refs[12]
    copies = [pltpu.make_async_copy(a, b, sem.at[i]) for i, (a, b) in enumerate(zip(sources, targets))]
    for copy in copies:
        copy.start()
    ld[0, 0] = refs[5][0, 0]
    for copy in copies:
        copy.wait()


def on_device(
    near_tiles, diag_tiles, near_index, near_mask, leaf_basis, level1_basis, level2_basis
):
    groups, leaves = lax.axis_size("grp"), lax.axis_size("leaf")
    hbm = pl.BlockSpec(memory_space=pltpu.HBM)
    vmem = pl.BlockSpec(memory_space=pltpu.VMEM)
    dma = pltpu.SemaphoreType.DMA
    shapes = (
        jax.ShapeDtypeStruct((2, RANK, RANK), f32),
        jax.ShapeDtypeStruct((1, RANK, RANK), f32),
        jax.ShapeDtypeStruct((RANK // 2, RANK), f32),
        jax.ShapeDtypeStruct((RANK // 2, RANK), f32),
        jax.ShapeDtypeStruct((RANK // 2, 4 * RANK), f32),
    )
    outs = pl.pallas_call(
        functools.partial(kernel, groups, leaves),
        out_shape=tuple(pltpu.VMEM(x.shape, f32) for x in shapes) + (pltpu.VMEM((1, RANK), f32),),
        in_specs=[hbm] * 7,
        out_specs=[vmem] * 6,
        scratch_shapes=[
            pltpu.VMEM((2 * NEAR, LEAF, LEAF), f32),
            pltpu.VMEM((2, LEAF, LEAF), f32),
            pltpu.VMEM((2, LEAF, LEAF), f32),
            pltpu.VMEM((LEAF, LEAF), f32),
            pltpu.VMEM((2, RANK, LEAF), f32),
            pltpu.VMEM((4, LEAF, LEAF), f32),
            pltpu.VMEM((4, LEAF, LEAF), f32),
            pltpu.VMEM((2, 2, LEAF, RANK), f32),
            pltpu.VMEM((2, LEAF, RANK), f32),
            pltpu.VMEM((9, 2, LEAF, RANK), f32),
            pltpu.VMEM((2, LEAF, RANK), f32),
            pltpu.VMEM((LEAF, RANK), f32),
            pltpu.VMEM((4, 2, LEAF, RANK), f32),
            pltpu.VMEM((2, RANK, LEAF), f32),
            pltpu.VMEM((2, RANK, RANK), f32),
            pltpu.VMEM((4, RANK, RANK), f32),
            pltpu.VMEM((4, RANK, RANK), f32),
            pltpu.VMEM((2, RANK, RANK), bf16),
            pltpu.VMEM((2, RANK, RANK), bf16),
            pltpu.VMEM((2, 2, RANK, RANK), f32),
            pltpu.VMEM((2, 4, RANK // 2, RANK), f32),
            pltpu.VMEM((4, RANK // 2, RANK), f32),
            pltpu.VMEM((RANK, 2 * RANK), f32),
            pltpu.VMEM((leaves, 1, RANK), f32),
            pltpu.VMEM((groups, 1, RANK), f32),
            pltpu.SMEM((2, NEAR), jnp.int32),
            pltpu.SMEM((2, NEAR), jnp.int32),
            dma((7,)),
            dma((12,)),
            dma((13,)),
            dma((leaves,)),
            dma((leaves,)),
            dma((groups,)),
            dma((groups,)),
            dma((4,)),
            dma((4,)),
        ],
        compiler_params=pltpu.CompilerParams(
            collective_id=0, has_side_effects=True, vmem_limit_bytes=66000000
        ),
    )(
        near_tiles.reshape(2 * NEAR, LEAF, LEAF),
        diag_tiles,
        leaf_basis,
        level1_basis,
        level2_basis,
        near_index,
        near_mask,
    )
    outs = pl.pallas_call(
        write_out,
        out_shape=(*shapes, jax.ShapeDtypeStruct((1, 1), f32)),
        in_specs=[vmem] * 6,
        out_specs=[hbm] * 5 + [pl.BlockSpec(memory_space=pltpu.SMEM)],
        scratch_shapes=[dma((5,))],
        compiler_params=pltpu.CompilerParams(vmem_limit_bytes=1 << 20),
    )(*outs)
    return (*outs[:5], outs[5].reshape(()))


def solution(mesh):
    in_specs = (
        P(AXES, None, None, None),
        P(AXES, None, None),
        P(AXES, None),
        P(AXES, None),
        P(AXES, None, None),
        P(AXES, None, None),
        P(AXES, None),
    )
    out_specs = (
        P(AXES, None, None),
        P(AXES, None, None),
        P(AXES, None),
        P(AXES, None),
        P(AXES, None),
        P(),
    )
    return jax.shard_map(
        on_device, mesh=mesh, in_specs=in_specs, out_specs=out_specs, check_vma=False
    )
```

```python
import functools

import jax
import jax.numpy as jnp
from jax import lax
from jax.experimental import pallas as pl
from jax.experimental.pallas import tpu as pltpu
from jax.sharding import PartitionSpec as P

LEAF = 256
RANK = 128
NEAR = 16
AXES = ("grp", "leaf")
f32 = jnp.float32
bf16 = jnp.bfloat16
MESH = pl.DeviceIdType.MESH


def split(x):
    hi = x.astype(bf16)
    return hi, (x - hi.astype(f32)).astype(bf16)


def dg(a, b, ca, cb):
    return lax.dot_general(
        a, b, (((ca,), (cb,)), ((), ())), preferred_element_type=f32
    )


def dot3(a, b, ca=1, cb=0):
    ah, al = split(a)
    bh, bl = split(b)
    return dg(ah, bh, ca, cb) + (dg(ah, bl, ca, cb) + dg(al, bh, ca, cb))


def rowb(x, j):
    return jnp.broadcast_to(x[j : j + 1, :], x.shape)


def lane(x, i):
    return jnp.take_along_axis(x, jnp.full((8, 128), i, jnp.int32), axis=1)


def rsqrt(d):
    s = lax.rsqrt(d)
    return s * (1.5 - (0.5 * d) * (s * s))


def halves(b):
    bh, bl = split(b)
    return jnp.concatenate([bh, bl], axis=1)


def dot3n(a, wide):
    ah, al = split(a)
    n = wide.shape[1] // 2
    both = dg(ah, wide, 1, 0)
    return both[:, :n] + (both[:, n:] + dg(al, wide[:, :n], 1, 0))


def eliminate(A, E, D, Zh, Zl, n, base, first=0, last=16, carry=None):
    ahead = n == 1
    row = lax.broadcasted_iota(jnp.int32, (8, 128), 0)
    col = lax.broadcasted_iota(jnp.int32, (8, 128), 1)

    def body(k, carry):
        kk = pl.multiple_of(8 * k, 8)
        kn = pl.multiple_of(8 * jnp.minimum(k + 1, 15), 8)
        before = 8 * jnp.maximum(k - 1, 0)
        now = jnp.logical_and(col >= kk, col < kk + 8)
        past = jnp.logical_and(col >= kk - 8, col < kk)
        past_all = jnp.broadcast_to(past[0:1, :], (RANK, RANK))
        unit = (col == row + kk).astype(f32)
        state = []
        for i in range(n):
            c, p = carry[i]
            if ahead:
                nxt = A[i, pl.ds(kn, 8), :]
            whole = A[i]
            hi, lo = split(whole)
            zh, zl = Zh[i], Zl[i]
            update = dg(hi, zh, 1, 0) + (dg(hi, zl, 1, 0) + dg(lo, zh, 1, 0))
            A[i] = jnp.where(past_all, 0.0, whole) - update
            if not ahead:
                nxt = A[i, pl.ds(kn, 8), :]
            cb = [lane(c, kk + j) for j in range(8)]
            if ahead:
                fb = [lane(nxt, before + j) for j in range(8)]
                nxt = jnp.where(past, 0.0, nxt)
                for j in range(8):
                    nxt = nxt - fb[j] * rowb(p, j)
            nb = [lane(nxt, kk + j) for j in range(8)]
            nxt = jnp.where(now, 0.0, nxt)
            x = jnp.where(now, unit, c)
            one = jnp.ones_like(c)
            state.append([x, nxt, cb, nb, x, one, one])
        for j in range(8):
            for i in range(n):
                x, nxt, cb, nb, v, d, rr = state[i]
                b = rowb(cb[j], j)
                r = pl.reciprocal(b, approx=True)
                e = 2.0 - b * r
                here = row == j
                m = jnp.where(here, 0.0, cb[j] * r) * e
                v = jnp.where(here, x, v)
                d = jnp.where(here, b, d)
                rr = jnp.where(here, r * e, rr)
                cb = [cb[q] - m * rowb(cb[q], j) if q > j else cb[q] for q in range(8)]
                x = x - m * rowb(x, j)
                state[i] = [x, nxt, cb, nb, v, d, rr]
        even = lax.rem(k, 2) == 0
        pair = pl.multiple_of(16 * (k // 2), 16)
        old = pl.multiple_of(16 * (jnp.maximum(k - 1, 0) // 2), 16)
        result = []
        for i in range(n):
            x, nxt, cb, nb, v, d, rr = state[i]
            p = x * rr
            for j in range(8):
                nxt = nxt - nb[j] * rowb(p, j)
            E[base + i, pl.ds(kk, 8), :] = v
            D[base + i, pl.ds(kk, 8), :] = d
            none = jnp.zeros((16, RANK), bf16)
            Zh[i, pl.ds(old, 16), :] = none
            Zl[i, pl.ds(old, 16), :] = none
            hi, lo = split(
                jnp.concatenate([jnp.where(even, p, 0.0), jnp.where(even, 0.0, p)], axis=0)
            )
            Zh[i, pl.ds(pair, 16), :] = hi
            Zl[i, pl.ds(pair, 16), :] = lo
            result.append((nxt, p))
        return tuple(result)

    if carry is None:
        Zh[...] = jnp.zeros_like(Zh)
        Zl[...] = jnp.zeros_like(Zl)
        zero = jnp.zeros((8, RANK), f32)
        carry = tuple((A[i, 0:8, :], zero) for i in range(n))
    return lax.fori_loop(first, last, body, carry)


def lower_mask():
    rows = lax.broadcasted_iota(jnp.int32, (RANK, RANK), 0)
    cols = lax.broadcasted_iota(jnp.int32, (RANK, RANK), 1)
    return cols <= rows


def lower_factor(E, y, i):
    product = lax.dot_general(
        y[i, :RANK, :RANK],
        E[i],
        (((1,), (1,)), ((), ())),
        precision=lax.Precision.HIGHEST,
        preferred_element_type=f32,
    )
    return jnp.where(lower_mask(), product, 0.0)


def reduced(E, D, y, i, basis_t):
    inverse = jnp.where(lower_mask(), E[i] * rsqrt(D[i]), 0.0)
    E[i] = inverse
    xh = dot3(
        inverse, jnp.concatenate([y[i, :RANK, RANK:], basis_t[:RANK]], axis=1)
    )
    sa = jnp.concatenate([y[i, RANK:, RANK:], basis_t[RANK:]], axis=1) - dot3(
        xh[:, :RANK], xh, 0, 0
    )
    return sa[:, :RANK], sa[:, RANK:]


def log_rows(d):
    return jnp.sum(jnp.log(d), axis=0, keepdims=True)


def block_system(s0, c01, c10, s1):
    return jnp.concatenate(
        [
            jnp.concatenate([s0, 0.5 * (c01 + c10.T)], axis=1),
            jnp.concatenate([0.5 * (c01.T + c10), s1], axis=1),
        ],
        axis=0,
    )


def kernel(
    groups,
    leaves,
    near,
    diag,
    leaf_basis,
    basis1,
    basis2,
    ids_hbm,
    mask_hbm,
    F0,
    F1,
    F2,
    S2,
    C2,
    LD,
    nv,
    dv,
    bv,
    b1v,
    wv,
    bt,
    yv,
    tu,
    us,
    win,
    zown,
    zsib,
    zu,
    at,
    A,
    E,
    D,
    Zh,
    Zl,
    ex,
    pp,
    pr,
    f2,
    la,
    lg,
    ids,
    mask,
    load_sem,
    send_sem,
    recv_sem,
    la_send,
    la_recv,
    lg_send,
    lg_recv,
    part_send,
    part_recv,
):
    count = groups * leaves
    g = lax.axis_index("grp")
    l = lax.axis_index("leaf")
    m = g * leaves + l
    par = lax.rem(m, 2)
    side = 2 * par - 1

    def device(k):
        return (k // leaves, lax.rem(k, leaves))

    def shifted(delta):
        return lax.rem(m + (delta + count), count)

    sibling = m - side

    loads = [
        pltpu.make_async_copy(leaf_basis, bv, load_sem.at[0]),
        pltpu.make_async_copy(basis1.at[0], b1v, load_sem.at[1]),
        pltpu.make_async_copy(basis2, wv.at[par], load_sem.at[2]),
        pltpu.make_async_copy(diag, dv, load_sem.at[3]),
        pltpu.make_async_copy(ids_hbm, ids, load_sem.at[4]),
        pltpu.make_async_copy(mask_hbm, mask, load_sem.at[5]),
        pltpu.make_async_copy(near, nv, load_sem.at[6]),
    ]
    for copy in loads[:3]:
        copy.start()

    barrier = pltpu.get_barrier_semaphore()
    direct = (-side, side, 4, -4)
    for delta in direct:
        pl.semaphore_signal(barrier, inc=1, device_id=device(shifted(delta)), device_id_type=MESH)

    def greet_leaf(t, _):
        pl.semaphore_signal(
            barrier, inc=1, device_id=(g, lax.rem(l + t, leaves)), device_id_type=MESH
        )
        return 0

    def greet_group(t, _):
        pl.semaphore_signal(
            barrier, inc=1, device_id=(lax.rem(g + t, groups), l), device_id_type=MESH
        )
        return 0

    lax.fori_loop(1, leaves, greet_leaf, 0)
    lax.fori_loop(1, groups, greet_group, 0)
    loads[3].start()

    for copy in loads[:3]:
        copy.wait()
    for copy in loads[4:]:
        copy.start()
    q2 = wv[par, :, RANK:]
    for b in range(2):
        t = dot3(bv[b, :, RANK:], b1v[b * RANK : (b + 1) * RANK, RANK:])
        tu[1, b] = t
        tu[0, b] = dot3(t, q2)

    loads[3].wait()
    for i in range(2):
        bt[i] = bv[i].T
        y = dot3(bt[i], dot3(dv[i], bv[i]))
        yv[i] = y
        A[i] = y[:RANK, :RANK]
    bt[2] = b1v[...].T

    carry = eliminate(A, E, D, Zh, Zl, 2, 0, 0, 4)
    pl.semaphore_wait(barrier, len(direct) + (leaves - 1) + (groups - 1))

    def remote(src, dst, sent, received, target):
        return pltpu.make_async_remote_copy(
            src_ref=src,
            dst_ref=dst,
            send_sem=send_sem.at[sent],
            recv_sem=recv_sem.at[received],
            device_id=device(target),
            device_id_type=MESH,
        )

    w_send = remote(wv.at[par], wv.at[par], 6, 9, sibling)
    sends = []
    for k, delta in enumerate(direct):
        source = tu.at[1] if k == 0 else tu.at[0]
        sends.append(remote(source, win.at[4 - delta], k, 4 - delta, shifted(delta)))
    sends[0].start()
    sends[1].start()
    w_send.start()
    for copy in sends[2:]:
        copy.start()

    eliminate(A, E, D, Zh, Zl, 2, 0, 4, 16, carry)
    for copy in loads[4:]:
        copy.wait()

    def near_block(a, j):
        slot = jnp.int32(0)
        live = f32(0.0)
        for t in range(NEAR):
            hit = jnp.logical_and(ids[a, t] == j, mask[a, t] == 1)
            slot = jnp.where(hit, t, slot)
            live = jnp.where(hit, f32(1.0), live)
        return nv[a * NEAR + slot], live

    schur = []
    for i in range(2):
        s, a_t = reduced(E, D, yv, i, bt[i])
        at[i] = a_t
        schur.append(s)
        tile, live = near_block(i, 2 * m + 1 - i)
        zown[i] = dot3n(tile, halves(bv[1 - i, :, RANK:])) * live

    system = block_system(schur[0], dot3(at[0], zown[0]), dot3(at[1], zown[1]), schur[1])
    y = dot3(bt[2], dot3(system, b1v[...]))
    yv[2] = y
    A[0] = y[:RANK, :RANK]

    def arrived(delta):
        slot = 4 + delta
        pltpu.make_async_copy(win.at[slot], win.at[slot], recv_sem.at[slot]).wait()

    eliminate(A, E, D, Zh, Zl, 1, 2)
    s, a1_t = reduced(E, D, yv, 2, bt[2])
    ex[par, 0] = s
    ex_sends = [remote(ex.at[par, i], ex.at[par, i], 9 + 2 * i, 10 + 2 * i, sibling) for i in range(2)]
    ex_sends[0].start()
    arrived(-side)

    right = [halves(win[4 - side, c]) for c in range(2)]
    for i in range(2):
        z = jnp.zeros((LEAF, RANK), f32)
        for c in range(2):
            tile, live = near_block(i, 2 * sibling + c)
            z = z + dot3n(tile, right[c]) * live
        zsib[i * RANK : (i + 1) * RANK] = dot3(at[i], z)

    ex[par, 1] = dot3(a1_t, zsib[...])
    ex_sends[1].start()
    arrived(side)
    relays = [
        remote(win.at[4 + side], win.at[4 - 3 * side], 4, 4 - 3 * side, shifted(4 * side)),
        remote(us, win.at[4 + 3 * side], 5, 4 + 3 * side, shifted(-4 * side)),
        remote(us, win.at[4 - 2 * side], 8, 4 - 2 * side, shifted(side)),
        remote(win.at[4 + side], win.at[4 + 2 * side], 7, 4 + 2 * side, sibling),
    ]
    relays[0].start()

    w_send.wait_recv()
    q2 = wv[1 - par, :, RANK:]
    for b in range(2):
        us[b] = dot3(win[4 - side, b], q2)
    relays[1].start()
    relays[2].start()
    zu[...] = jnp.zeros_like(zu)
    w = jnp.concatenate([wv[0], wv[1]], axis=0)
    bt[3] = w.T

    def far(delta):
        e = (par + delta + 8) // 2 - 4
        slot_e = jnp.where(e < 0, e + 2, e + 1)
        right = [halves(win[4 + delta, b]) for b in range(2)]
        for a in range(2):
            z = zu[slot_e, a]
            for b in range(2):
                tile, live = near_block(a, 2 * (m + delta) + b)
                z = z + dot3n(tile, right[b]) * live
            zu[slot_e, a] = z

    far(side)
    arrived(-4 * side)
    far(-4 * side)
    for i in range(2):
        F0[i] = lower_factor(E, yv, i)
    F1[0] = lower_factor(E, yv, 2)
    logs = log_rows(D[0]) + log_rows(D[1]) + log_rows(D[2])

    for copy in ex_sends:
        copy.wait_recv()
    relays[3].start()
    system = block_system(ex[0, 0], ex[0, 1], ex[1, 1], ex[1, 0])
    y = dot3(bt[3], dot3(system, w))
    yv[3] = y
    A[0] = y[:RANK, :RANK]
    eliminate(A, E, D, Zh, Zl, 1, 3)
    logs = logs + log_rows(D[3]) * jnp.where(par == 0, 1.0, 0.0)
    la[l] = logs

    def to_leaf(t, wait):
        copy = pltpu.make_async_remote_copy(
            src_ref=la.at[l],
            dst_ref=la.at[l],
            send_sem=la_send.at[t],
            recv_sem=la_recv.at[t],
            device_id=(g, lax.rem(l + t, leaves)),
            device_id_type=MESH,
        )
        if wait:
            copy.wait()
        else:
            copy.start()

    def to_group(t, wait):
        copy = pltpu.make_async_remote_copy(
            src_ref=lg.at[g],
            dst_ref=lg.at[g],
            send_sem=lg_send.at[t],
            recv_sem=lg_recv.at[t],
            device_id=(lax.rem(g + t, groups), l),
            device_id_type=MESH,
        )
        if wait:
            copy.wait()
        else:
            copy.start()

    def each(size, step, wait):
        def body(t, _):
            step(t, wait)
            return 0

        lax.fori_loop(size // 2 - 1, size, body, 0)
        lax.fori_loop(1, size // 2 - 1, body, 0)

    each(leaves, to_leaf, False)
    s, a2_t = reduced(E, D, yv, 3, bt[3])
    half = pl.multiple_of(par * (RANK // 2), RANK // 2)
    f2[:, :RANK] = lower_factor(E, yv, 3)
    f2[:, RANK:] = s
    F2[...] = f2[pl.ds(half, RANK // 2), :RANK]
    S2[...] = f2[pl.ds(half, RANK // 2), RANK:]
    chain = dot3(jnp.where(par == 0, a2_t[:, :RANK], a2_t[:, RANK:]), a1_t)

    def reduce_part(e):
        i = jnp.where(e < 0, e + 2, e + 1)
        below = jnp.concatenate([dot3(at[a], zu[i, a]) for a in range(2)], axis=0)
        part = dot3(chain, below)
        pp[0, i] = part[: RANK // 2]
        pp[1, i] = part[RANK // 2 :]
        copy = pltpu.make_async_remote_copy(
            src_ref=pp.at[1 - par, i],
            dst_ref=pr.at[i],
            send_sem=part_send.at[i],
            recv_sem=part_recv.at[i],
            device_id=device(sibling),
            device_id_type=MESH,
        )
        copy.start()
        return copy

    parts = [reduce_part(-2 * side)]
    arrived(-3 * side)
    far(-3 * side)
    arrived(-2 * side)
    far(-2 * side)
    parts.append(reduce_part(-side))
    arrived(4 * side)
    far(4 * side)
    each(leaves, to_leaf, True)
    lg[g] = jnp.sum(la[...], axis=0)
    each(groups, to_group, False)
    arrived(3 * side)
    far(3 * side)
    parts.append(reduce_part(2 * side))
    arrived(2 * side)
    far(2 * side)
    parts.append(reduce_part(side))
    for copy in sends:
        copy.wait_send()
    w_send.wait_send()
    for copy in ex_sends:
        copy.wait_send()
    for copy in relays:
        copy.wait_send()
    for copy in parts:
        copy.wait()
    for i in range(4):
        C2[:, i * RANK : (i + 1) * RANK] = pp[par, i] + pr[i]
    each(groups, to_group, True)
    LD[...] = jnp.sum(lg[...], axis=0)


def write_out(*refs):
    sources, targets, ld, sem = refs[:5], refs[6:11], refs[11], refs[12]
    copies = [pltpu.make_async_copy(a, b, sem.at[i]) for i, (a, b) in enumerate(zip(sources, targets))]
    for copy in copies:
        copy.start()
    ld[0, 0] = refs[5][0, 0]
    for copy in copies:
        copy.wait()


def on_device(
    near_tiles, diag_tiles, near_index, near_mask, leaf_basis, level1_basis, level2_basis
):
    groups, leaves = lax.axis_size("grp"), lax.axis_size("leaf")
    hbm = pl.BlockSpec(memory_space=pltpu.HBM)
    vmem = pl.BlockSpec(memory_space=pltpu.VMEM)
    dma = pltpu.SemaphoreType.DMA
    shapes = (
        jax.ShapeDtypeStruct((2, RANK, RANK), f32),
        jax.ShapeDtypeStruct((1, RANK, RANK), f32),
        jax.ShapeDtypeStruct((RANK // 2, RANK), f32),
        jax.ShapeDtypeStruct((RANK // 2, RANK), f32),
        jax.ShapeDtypeStruct((RANK // 2, 4 * RANK), f32),
    )
    outs = pl.pallas_call(
        functools.partial(kernel, groups, leaves),
        out_shape=tuple(pltpu.VMEM(x.shape, f32) for x in shapes) + (pltpu.VMEM((1, RANK), f32),),
        in_specs=[hbm] * 7,
        out_specs=[vmem] * 6,
        scratch_shapes=[
            pltpu.VMEM((2 * NEAR, LEAF, LEAF), f32),
            pltpu.VMEM((2, LEAF, LEAF), f32),
            pltpu.VMEM((2, LEAF, LEAF), f32),
            pltpu.VMEM((LEAF, LEAF), f32),
            pltpu.VMEM((2, RANK, LEAF), f32),
            pltpu.VMEM((4, LEAF, LEAF), f32),
            pltpu.VMEM((4, LEAF, LEAF), f32),
            pltpu.VMEM((2, 2, LEAF, RANK), f32),
            pltpu.VMEM((2, LEAF, RANK), f32),
            pltpu.VMEM((9, 2, LEAF, RANK), f32),
            pltpu.VMEM((2, LEAF, RANK), f32),
            pltpu.VMEM((LEAF, RANK), f32),
            pltpu.VMEM((4, 2, LEAF, RANK), f32),
            pltpu.VMEM((2, RANK, LEAF), f32),
            pltpu.VMEM((2, RANK, RANK), f32),
            pltpu.VMEM((4, RANK, RANK), f32),
            pltpu.VMEM((4, RANK, RANK), f32),
            pltpu.VMEM((2, RANK, RANK), bf16),
            pltpu.VMEM((2, RANK, RANK), bf16),
            pltpu.VMEM((2, 2, RANK, RANK), f32),
            pltpu.VMEM((2, 4, RANK // 2, RANK), f32),
            pltpu.VMEM((4, RANK // 2, RANK), f32),
            pltpu.VMEM((RANK, 2 * RANK), f32),
            pltpu.VMEM((leaves, 1, RANK), f32),
            pltpu.VMEM((groups, 1, RANK), f32),
            pltpu.SMEM((2, NEAR), jnp.int32),
            pltpu.SMEM((2, NEAR), jnp.int32),
            dma((7,)),
            dma((12,)),
            dma((13,)),
            dma((leaves,)),
            dma((leaves,)),
            dma((groups,)),
            dma((groups,)),
            dma((4,)),
            dma((4,)),
        ],
        compiler_params=pltpu.CompilerParams(
            collective_id=0, has_side_effects=True, vmem_limit_bytes=66000000
        ),
    )(
        near_tiles.reshape(2 * NEAR, LEAF, LEAF),
        diag_tiles,
        leaf_basis,
        level1_basis,
        level2_basis,
        near_index,
        near_mask,
    )
    outs = pl.pallas_call(
        write_out,
        out_shape=(*shapes, jax.ShapeDtypeStruct((1, 1), f32)),
        in_specs=[vmem] * 6,
        out_specs=[hbm] * 5 + [pl.BlockSpec(memory_space=pltpu.SMEM)],
        scratch_shapes=[dma((5,))],
        compiler_params=pltpu.CompilerParams(vmem_limit_bytes=1 << 20),
    )(*outs)
    return (*outs[:5], outs[5].reshape(()))


def solution(mesh):
    in_specs = (
        P(AXES, None, None, None),
        P(AXES, None, None),
        P(AXES, None),
        P(AXES, None),
        P(AXES, None, None),
        P(AXES, None, None),
        P(AXES, None),
    )
    out_specs = (
        P(AXES, None, None),
        P(AXES, None, None),
        P(AXES, None),
        P(AXES, None),
        P(AXES, None),
        P(),
    )
    return jax.shard_map(
        on_device, mesh=mesh, in_specs=in_specs, out_specs=out_specs, check_vma=False
    )
```
